512 devices in a mesh: frame: 16 (over z_lo, core), band: 32 (over y, z_hi, x).
Axes of the slice: x: 4, y: 4, z: 16 (z_hi: 2, z_lo: 8; z = z_hi * 8 + z_lo), core: 2. Of those that a mesh axis runs over, the one named last changes fastest.
Arguments:
- noisy_snapshot_stack: bfloat16 [16, 32, 180, 512], P('frame', 'band'), may hold values from -6 to 6
- gaussian_perturbation: bfloat16 [16, 32, 180, 512], P('frame', 'band'), may hold values from -6 to 6
- snapshot_noise_indices: int32 [16], P('frame'), may hold values from 0 to 15, each once
- partition_longitude_starts: int32 [16], P('frame'), may hold values from 0 to 59
- latitude_patch_tally: int32 [32], replicated, may hold values from 90 to 180
- normalizer_scaling: float32 [512], replicated, may hold values from 0.1 to 1.9
- head_score_scales: float32 [2, 8], replicated, may hold values from 0.5 to 100
- local_projection_matrices: bfloat16 [512, 1536], P(None, 'band'), may hold values from -0.25 to 0.25
- time_projection_matrices: bfloat16 [512, 1536], P(None, 'band'), may hold values from -0.25 to 0.25
- final_projection_matrices: bfloat16 [1024, 512], P(None, 'band'), may hold values from -0.1875 to 0.1875
Outputs:
- next_state: bfloat16 [16, 32, 180, 512], P('frame', 'band')
The draws below stay inside these ranges and needn't reach their ends.
Inputs may be any that keep to these rules, and one draw needn't show every extreme that they name: `snapshot_noise_indices`: each level index 0 to 15 belongs to exactly one frame.
All inputs are finite; a program needn't handle non-finite values.
Results may differ from the reference program's by a relative error of at most 0.0071.
Values may be sent and summed in bfloat16 or wider, within the bound.
A program may use at most 64 MiB of HBM per device.

```python
import math
import jax
import jax.numpy as jnp
from jax import lax

PATCH_BREADTH = 512
HEADS = 8
HEAD_DIM = 64
LON = 180
WINDOW = 60
PRIOR_SNAPSHOTS = 3
RB = 1
FRAMES = 16
LAT = 32
NBANDS = 32


def draw_head_score_scales(key, part):
    spread = jax.random.uniform(key, (2, HEADS), jnp.float32)
    return 0.5 * jnp.exp(spread * jnp.log(8.0))


def set_ends(values, key, least, high):
    shape = values.shape
    spot = [jax.random.randint(jax.random.fold_in(key, axis), (), 0, shape[axis]) for axis in range(len(shape))]
    values = values.at[tuple(spot)].set(least)
    longest = shape.index(max(shape))
    spot[longest] = (spot[longest] + 1) % shape[longest]
    return values.at[tuple(spot)].set(high)


def block_scale(stream_key, shape, pieces, smallest, top_value):
    loudness = 1.0
    for position, parts in pieces:
        draws = jax.random.uniform(jax.random.fold_in(jax.random.fold_in(stream_key, 6), position), (parts,), jnp.float32, smallest / len(pieces), top_value / len(pieces))
        loudness = loudness * jnp.repeat(jnp.exp(draws), shape[position] // parts).reshape((-1,) + (1,) * (len(shape) - 1 - position))
    return loudness


def noise(own_key, dims, width, most, pieces=(), kind=jnp.bfloat16):
    loudness = block_scale(own_key, dims, pieces, -0.22, 0.18) if pieces else 1.0
    entries = jax.random.normal(own_key, dims, jnp.float32) * width * loudness
    return jnp.minimum(jnp.maximum(entries, -most), most).astype(kind)


def setup_inputs(seed: int = 0) -> dict:
    seeds = jax.random.split(jax.random.key(seed), 11)
    return {
        "noisy_snapshot_stack": noise(seeds[0], (FRAMES, LAT, LON, PATCH_BREADTH), 1.0, 6.0, ((0, 16), (1, 32))),
        "gaussian_perturbation": noise(seeds[1], (FRAMES, LAT, LON, PATCH_BREADTH), 1.0, 6.0, ((0, 16), (1, 32))),
        "snapshot_noise_indices": jax.random.permutation(seeds[2], FRAMES).astype(jnp.int32),
        "partition_longitude_starts": set_ends(jax.random.randint(seeds[3], (FRAMES,), 0, WINDOW), jax.random.fold_in(seeds[3], 1), 0, WINDOW - 1).astype(jnp.int32),
        "latitude_patch_tally": set_ends(jax.random.randint(seeds[4], (NBANDS,), LON * RB // 2, LON * RB + 1), jax.random.fold_in(seeds[4], 1), LON * RB // 2, LON * RB).astype(jnp.int32),
        "normalizer_scaling": jnp.clip(1.0 + 0.18 * jax.random.normal(seeds[5], (PATCH_BREADTH,), jnp.float32), 0.1, 1.9),
        "head_score_scales": draw_head_score_scales(jax.random.fold_in(seeds[10], 71), 0),
        "local_projection_matrices": noise(seeds[7], (PATCH_BREADTH, 3 * PATCH_BREADTH), PATCH_BREADTH ** -0.5, 0.25, ((1, 32),)),
        "time_projection_matrices": noise(seeds[8], (PATCH_BREADTH, 3 * PATCH_BREADTH), PATCH_BREADTH ** -0.5, 0.25, ((1, 32),)),
        "final_projection_matrices": noise(seeds[9], (2 * PATCH_BREADTH, PATCH_BREADTH), (2 * PATCH_BREADTH) ** -0.5, 0.1875, ((1, 32),)),
    }


epsilon = 1e-06
sigma_low = 0.1
sigma_high = 2.0
keep_share = 0.8
fresh_share = 0.6

def sigma_of(level):
    return sigma_low * jnp.power(sigma_high / sigma_low, (level.astype(jnp.float32) + 1.0) / FRAMES)

def unit_heads(content_vectors):
    shaped = content_vectors.reshape(content_vectors.shape[:-1] + (HEADS, HEAD_DIM))
    scale = lax.rsqrt(lax.optimization_barrier(jnp.mean(shaped * shaped, axis=-1, keepdims=True)) + epsilon)
    return (shaped * scale).reshape(content_vectors.shape)

def project(frame, weight):
    rows, lon, token_extent = frame.shape
    out = jnp.dot(frame.reshape(-1, token_extent), weight, preferred_element_type=jnp.float32)
    asking_vectors = unit_heads(out[:, :token_extent]).astype(jnp.bfloat16).reshape(rows, lon, token_extent)
    key = unit_heads(out[:, token_extent:2 * token_extent]).astype(jnp.bfloat16).reshape(rows, lon, token_extent)
    value = out[:, 2 * token_extent:].astype(jnp.bfloat16).reshape(rows, lon, token_extent)
    return (asking_vectors, key, value)

def local_patch_mixer(asking_vectors, fringe_lookup_vectors, fringe_content_vectors, fringe_present_flags, snapshot_longitude_shift, temper):
    rows, lon, token_extent = asking_vectors.shape
    wins = lon // WINDOW
    asking_vectors = jnp.roll(asking_vectors, -snapshot_longitude_shift, axis=1).reshape(rows, wins, WINDOW, HEADS, HEAD_DIM)
    fringe_lookup_vectors = jnp.roll(fringe_lookup_vectors, -snapshot_longitude_shift, axis=1).reshape(rows + 2, wins, WINDOW, HEADS, HEAD_DIM)
    fringe_content_vectors = jnp.roll(fringe_content_vectors, -snapshot_longitude_shift, axis=1).reshape(rows + 2, wins, WINDOW, HEADS, HEAD_DIM)
    fringe_present_flags = jnp.roll(fringe_present_flags, -snapshot_longitude_shift, axis=1).reshape(rows + 2, wins, WINDOW)
    lookup_vectors = jnp.concatenate([fringe_lookup_vectors[:-2], fringe_lookup_vectors[1:-1], fringe_lookup_vectors[2:]], axis=2)
    content_vectors = jnp.concatenate([fringe_content_vectors[:-2], fringe_content_vectors[1:-1], fringe_content_vectors[2:]], axis=2)
    permitted_mask = jnp.concatenate([fringe_present_flags[:-2], fringe_present_flags[1:-1], fringe_present_flags[2:]], axis=2)
    inner = jnp.arange(WINDOW)
    middle = jnp.arange(3 * WINDOW)
    itself = middle[None, :] == inner[:, None] + WINDOW
    permitted_mask = permitted_mask[:, :, None, None, :] | itself[None, None, None]
    scores = jnp.einsum('rwqhd,rwkhd->rwhqk', asking_vectors.astype(jnp.float32), lookup_vectors.astype(jnp.float32))
    scores = scores * (temper / math.sqrt(HEAD_DIM))[None, None, :, None, None]
    top = lax.optimization_barrier(jnp.max(jnp.where(permitted_mask, scores, -jnp.inf), axis=-1, keepdims=True))
    weights = jnp.where(permitted_mask, jnp.exp(scores - top), 0.0)
    probs = (weights / lax.optimization_barrier(jnp.sum(weights, axis=-1, keepdims=True))).astype(jnp.bfloat16)
    combined_result_field = jnp.einsum('rwhqk,rwkhd->rwqhd', probs.astype(jnp.float32), content_vectors.astype(jnp.float32))
    combined_result_field = combined_result_field.reshape(rows, lon, token_extent)
    return jnp.roll(combined_result_field, snapshot_longitude_shift, axis=1).astype(jnp.bfloat16)

def across_time_mixer(asking_vectors, lookup_vectors, content_vectors, permitted_mask, temper):
    count, token_extent = asking_vectors.shape
    span = lookup_vectors.shape[0]
    query_heads = asking_vectors.astype(jnp.float32).reshape(count, HEADS, HEAD_DIM)
    key_heads = lookup_vectors.astype(jnp.float32).reshape(span, count, HEADS, HEAD_DIM)
    value_heads = content_vectors.astype(jnp.float32).reshape(span, count, HEADS, HEAD_DIM)
    scores = jnp.einsum('thd,jthd->jht', query_heads, key_heads)
    scores = scores * (temper / math.sqrt(HEAD_DIM))[None, :, None]
    top = lax.optimization_barrier(jnp.max(jnp.where(permitted_mask, scores, -jnp.inf), axis=0, keepdims=True))
    weights = jnp.where(permitted_mask, jnp.exp(scores - top), 0.0)
    probs = (weights / lax.optimization_barrier(jnp.sum(weights, axis=0, keepdims=True))).astype(jnp.bfloat16)
    combined_result_field = jnp.einsum('jht,jthd->thd', probs.astype(jnp.float32), value_heads)
    return combined_result_field.reshape(count, token_extent).astype(jnp.bfloat16)

def reference(noisy_snapshot_stack, gaussian_perturbation, snapshot_noise_indices, partition_longitude_starts, latitude_patch_tally, normalizer_scaling, head_score_scales, local_projection_matrices, time_projection_matrices, final_projection_matrices):
    state_f = noisy_snapshot_stack.astype(jnp.float32)
    normed = (state_f * lax.rsqrt(lax.optimization_barrier(jnp.mean(state_f * state_f, axis=-1, keepdims=True)) + epsilon) * normalizer_scaling).astype(jnp.bfloat16)
    row_ids = jnp.arange(LAT).astype(jnp.int32)
    band_of = row_ids // RB
    inner = (row_ids % RB)[:, None] * LON + jnp.arange(LON).astype(jnp.int32)[None, :]
    band_ids = jnp.arange(NBANDS).astype(jnp.int32)
    band_count = lax.optimization_barrier(jnp.sum(jnp.where(band_of[:, None] == band_ids[None, :], latitude_patch_tally[None, :], 0), axis=1))
    valid = inner < band_count[:, None]
    fringe_present_flags = jnp.pad(valid, ((1, 1), (0, 0)))

    def space_frame(args):
        frame, snapshot_longitude_shift = args
        asking_vectors, key, value = project(frame, local_projection_matrices)
        fringe_lookup_vectors = jnp.pad(key, ((1, 1), (0, 0), (0, 0)))
        fringe_content_vectors = jnp.pad(value, ((1, 1), (0, 0), (0, 0)))
        return local_patch_mixer(asking_vectors, fringe_lookup_vectors, fringe_content_vectors, fringe_present_flags, snapshot_longitude_shift, head_score_scales[0])
    space_mix = lax.map(space_frame, (normed, partition_longitude_starts))
    temporal_queries, time_key, time_value = lax.map(lambda frame: project(frame, time_projection_matrices), normed)
    padding = jnp.zeros((PRIOR_SNAPSHOTS, LAT, LON, PATCH_BREADTH), jnp.bfloat16)
    keys_all = jnp.concatenate([padding, time_key], axis=0)
    values_all = jnp.concatenate([padding, time_value], axis=0)
    frame_ids = jnp.arange(FRAMES).astype(jnp.int32)

    def time_frame(args):
        asking_vectors, index = args
        lookup_vectors = lax.dynamic_slice_in_dim(keys_all, index, PRIOR_SNAPSHOTS + 1, 0)
        content_vectors = lax.dynamic_slice_in_dim(values_all, index, PRIOR_SNAPSHOTS + 1, 0)
        allowed_pair_flags = index - PRIOR_SNAPSHOTS + jnp.arange(PRIOR_SNAPSHOTS + 1).astype(jnp.int32) >= 0
        combined_result_field = across_time_mixer(asking_vectors.reshape(-1, PATCH_BREADTH), lookup_vectors.reshape(PRIOR_SNAPSHOTS + 1, -1, PATCH_BREADTH), content_vectors.reshape(PRIOR_SNAPSHOTS + 1, -1, PATCH_BREADTH), allowed_pair_flags[:, None, None], head_score_scales[1])
        return combined_result_field.reshape(LAT, LON, PATCH_BREADTH)
    time_mix = lax.map(time_frame, (temporal_queries, frame_ids))
    mixed = jnp.concatenate([space_mix, time_mix], axis=-1).reshape(-1, 2 * PATCH_BREADTH)
    update = jnp.dot(mixed, final_projection_matrices, preferred_element_type=jnp.float32).reshape(FRAMES, LAT, LON, PATCH_BREADTH)
    sigma = sigma_of(snapshot_noise_indices)[:, None, None, None]
    sigma_next = sigma_of(snapshot_noise_indices - 1)[:, None, None, None]
    denoised = state_f / (1.0 + sigma * sigma) + sigma * lax.rsqrt(1.0 + sigma * sigma) * update
    noise_f = gaussian_perturbation.astype(jnp.float32)
    stepped = denoised + sigma_next * (keep_share * (state_f - denoised) / sigma + fresh_share * noise_f)
    finished = (snapshot_noise_indices == 0)[:, None, None, None]
    return jnp.where(finished, sigma_high * noise_f, stepped).astype(jnp.bfloat16)
```

```python
import math

import jax
import jax.numpy as jnp
from jax import lax
from jax.experimental import pallas as pl
from jax.experimental.pallas import tpu as pltpu
from jax.sharding import PartitionSpec as P

MESH = pl.DeviceIdType.MESH
HEADS = 8
LON = 180
WINDOW = 60
ROWS = 192
D = 512
SHARD = 64
QKV = 48
BIG = -1e30
epsilon = 1e-06
f32 = jnp.float32
bf16 = jnp.bfloat16

LAT_UP, LAT_DOWN, TIME_Z, TIME_SIB, TIME_FWD, TIME_RELAY, W_Z = range(7)
STREAM0 = 7
PER_STREAM = 12
SLOTS = STREAM0 + 4 * PER_STREAM


def nt_dot(a, b):
    return lax.dot_general(a, b, (((1,), (1,)), ((), ())), preferred_element_type=f32)


def head_sums(x, bd):
    hi = x.astype(bf16)
    lo = (x - hi.astype(f32)).astype(bf16)
    return jnp.dot(hi, bd, preferred_element_type=f32) + jnp.dot(
        lo, bd, preferred_element_type=f32
    )


def head_sums_all(x, bd):
    return jnp.concatenate(
        [head_sums(x[:, 256 * i : 256 * i + 256], bd) for i in range(2)], axis=1
    )


def unit(u, bd):
    mean = head_sums_all(u * u, bd) * (1.0 / 64)
    return (u * lax.rsqrt(mean + epsilon)).astype(bf16)


def coords():
    f = lax.axis_index("frame")
    b = lax.axis_index("band")
    return f, b, f // 2, f % 2, b // 8, (b // 4) % 2, b % 4


def kernel(
    level,
    starts,
    tally,
    temper,
    state,
    noise,
    gain,
    local_w,
    time_w,
    final_w,
    out,
    G,
    hist,
    lat,
    xn,
    kbuf,
    vext,
    bias,
    ssem,
    rsem,
):
    f, b, zl, c, y, zh, x = coords()
    oc = 1 - c

    @pl.when(c == 0)
    def _():
        G[0, y, zh, x, 0:QKV, :] = local_w[...].T
        G[0, y, zh, x, QKV:SHARD, :] = final_w[0:D, :].T

    @pl.when(c == 1)
    def _():
        G[1, y, zh, x, 0:QKV, :] = time_w[...].T
        G[1, y, zh, x, QKV:SHARD, :] = final_w[D : 2 * D, :].T

    def at(dx=0, dy=0, dzl=0, cc=None, zhh=None):
        yy = (y + dy + 4) % 4
        xx = (x + dx + 4) % 4
        z2 = zh if zhh is None else zhh
        c2 = c if cc is None else cc
        return {"frame": (zl + dzl) * 2 + c2, "band": (yy * 2 + z2) * 4 + xx}

    sibling = at(cc=oc)
    xr, xl, yr, yl = at(dx=1), at(dx=-1), at(dy=1), at(dy=-1)
    across = at(zhh=1 - zh)
    z_next, z_prev = at(dzl=1), at(dzl=-1)
    relay_to, relay_from = at(dzl=1, cc=0), at(dzl=-1, cc=1)
    up = {"frame": f, "band": b - 1}
    down = {"frame": f, "band": b + 1}

    has_prev, has_next = zl > 0, zl < 7
    has_up, has_down = b > 0, b < 31
    relays = (c == 1) & has_next
    relayed = (c == 0) & has_prev

    barrier = pltpu.get_barrier_semaphore()

    def greet(dev):
        pl.semaphore_signal(barrier, inc=1, device_id=dev, device_id_type=MESH)

    for dev in (sibling, xr, xl, yr, yl, across):
        greet(dev)
    optional = (
        (has_next, z_next),
        (has_prev, z_prev),
        (relays, relay_to),
        (relayed, relay_from),
        (has_up, up),
        (has_down, down),
    )
    count = 6
    for cond, dev in optional:
        pl.when(cond)(lambda dev=dev: greet(dev))
        count = count + jnp.where(cond, 1, 0)
    pl.semaphore_wait(barrier, count)

    def copy(src, dst, slot, dev):
        return pltpu.make_async_remote_copy(
            src_ref=src,
            dst_ref=dst,
            send_sem=ssem.at[slot],
            recv_sem=rsem.at[slot],
            device_id=dev,
            device_id_type=MESH,
        )

    def gref(cc, yy, zz, xx, r0, r1):
        return G.at[cc, yy, zz, xx, pl.ds(r0, r1 - r0), :]

    own = gref(c, y, zh, x, 0, SHARD)
    z_in = gref(c, y, 1 - zh, x, 0, SHARD)
    copy(own, own, W_Z, across).start()
    lat_to_down = copy(state, lat.at[0], LAT_DOWN, down)
    lat_to_up = copy(state, lat.at[1], LAT_UP, up)
    pl.when(has_down)(lat_to_down.start)
    pl.when(has_up)(lat_to_up.start)
    time_z = copy(state, hist.at[1], TIME_Z, z_next)
    pl.when(has_next)(time_z.start)
    time_sib = copy(state, hist.at[0], TIME_SIB, sibling)
    pl.when(c == 0)(time_sib.start)

    def ref_x(row_y, zz, xx, r0, r1):
        return gref(c, row_y, zz, xx, r0, r1)

    class Stream:
        def __init__(self, index, zz, order):
            self.s = STREAM0 + PER_STREAM * index
            self.zz, self.order = zz, order
            self.r0, self.r1 = (0, 32) if order == 0 else (32, 64)
            self.first = (xr, xl) if order == 0 else (yr, yl)
            self.second = (yr, yl) if order == 0 else (xr, xl)

        def one(self, d, r0=None, r1=None):
            r0 = self.r0 if r0 is None else r0
            r1 = self.r1 if r1 is None else r1
            if self.order == 0:
                return G.at[c, y, self.zz, (x + d + 4) % 4, pl.ds(r0, r1 - r0), :]
            return G.at[c, (y + d + 4) % 4, self.zz, x, pl.ds(r0, r1 - r0), :]

        def line(self, d, cc=None, r0=None, r1=None):
            r0 = self.r0 if r0 is None else r0
            r1 = self.r1 if r1 is None else r1
            cc = c if cc is None else cc
            if self.order == 0:
                return G.at[cc, (y + d + 4) % 4, self.zz, :, pl.ds(r0, r1 - r0), :]
            return G.at[cc, :, self.zz, (x + d + 4) % 4, pl.ds(r0, r1 - r0), :]

        def go(self, ref, slot, dev):
            copy(ref, ref, self.s + slot, dev).start()

        def got(self, ref, slot):
            copy(ref, ref, self.s + slot, sibling).wait_recv()

        def sent(self, ref, slot):
            copy(ref, ref, self.s + slot, sibling).wait_send()

        def step1(self):
            self.go(self.one(0), 0, self.first[0])
            self.go(self.one(0), 1, self.first[1])

        def step2(self):
            mid = self.r0 + 16
            self.got(self.one(-1), 0)
            self.go(self.one(-1, self.r0, mid), 2, self.first[0])
            self.got(self.one(1), 1)
            self.go(self.one(1, mid, self.r1), 3, self.first[1])

        def step3(self):
            mid = self.r0 + 16
            self.got(self.one(2, self.r0, mid), 2)
            self.got(self.one(2, mid, self.r1), 3)
            self.go(self.line(0), 4, self.second[0])
            self.go(self.line(0), 5, self.second[1])
            self.go(self.line(0), 8, sibling)

        def step4(self):
            mid = self.r0 + 16
            self.got(self.line(-1), 4)
            self.go(self.line(-1, None, self.r0, mid), 6, self.second[0])
            self.go(self.line(-1), 9, sibling)
            self.got(self.line(1), 5)
            self.go(self.line(1, None, mid, self.r1), 7, self.second[1])
            self.go(self.line(1), 10, sibling)

        def step5(self):
            mid = self.r0 + 16
            self.got(self.line(2, None, self.r0, mid), 6)
            self.got(self.line(2, None, mid, self.r1), 7)
            self.go(self.line(2), 11, sibling)

        def finish(self):
            mid = self.r0 + 16
            for i, d in enumerate((0, -1, 1, 2)):
                self.got(self.line(d, oc), 8 + i)
            self.sent(self.one(0), 0)
            self.sent(self.one(0), 1)
            self.sent(self.one(0, self.r0, mid), 2)
            self.sent(self.one(0, mid, self.r1), 3)
            self.sent(self.line(0), 4)
            self.sent(self.line(0), 5)
            self.sent(self.line(0, None, self.r0, mid), 6)
            self.sent(self.line(0, None, mid, self.r1), 7)
            for i, d in enumerate((0, -1, 1, 2)):
                self.sent(self.line(d), 8 + i)

    streams = [
        Stream(0, zh, 0),
        Stream(1, zh, 1),
        Stream(2, 1 - zh, 0),
        Stream(3, 1 - zh, 1),
    ]
    mine, theirs = streams[:2], streams[2:]
    for s in mine:
        s.step1()

    def normalize(i, row_ref):
        s = row_ref[...].astype(f32)
        r = lax.rsqrt(jnp.mean(s * s, axis=-1, keepdims=True) + epsilon)
        xn[i, 0:LON, :] = (s * r * gain[...]).astype(bf16)
        xn[i, LON:ROWS, :] = jnp.zeros((ROWS - LON, D), bf16)

    normalize(0, state)

    for s in mine:
        s.step2()

    shift = starts[0]
    qi = lax.broadcasted_iota(jnp.int32, (ROWS, ROWS), 0)
    ki = lax.broadcasted_iota(jnp.int32, (ROWS, ROWS), 1)

    def window(i):
        d = i - shift
        d = jnp.where(d < 0, d + LON, d)
        return jnp.where(d >= WINDOW, 1, 0) + jnp.where(d >= 2 * WINDOW, 1, 0)

    same = window(qi) == window(ki)
    n_above = jnp.where(has_up, tally[jnp.maximum(b - 1, 0)], 0)
    n_below = jnp.where(has_down, tally[jnp.minimum(b + 1, 31)], 0)
    n_own = tally[b]
    for i, n in enumerate((n_own, n_above, n_below)):
        seen = same & (ki < n)
        if i == 0:
            seen = seen | (qi == ki)
        bias[i] = jnp.where(seen, 0.0, BIG)

    for s in mine:
        s.step3()
    for s in mine:
        s.step4()

    @pl.when(has_prev)
    def _():
        copy(state, hist.at[1], TIME_Z, sibling).wait_recv()

        @pl.when(c == 1)
        def _():
            copy(hist.at[1], hist.at[0], TIME_FWD, sibling).start()

        @pl.when(c == 0)
        def _():
            copy(hist.at[1], hist.at[2], TIME_FWD, sibling).start()

        @pl.when(relays)
        def _():
            copy(hist.at[1], hist.at[2], TIME_RELAY, relay_to).start()

    copy(z_in, z_in, W_Z, sibling).wait_recv()
    for s in theirs:
        s.step1()
    for s in mine:
        s.step5()
    for s in theirs:
        s.step2()
    for s in theirs:
        s.step3()

    @pl.when(c == 1)
    def _():
        copy(state, hist.at[0], TIME_SIB, sibling).wait_recv()

    @pl.when(has_prev)
    def _():
        @pl.when(c == 0)
        def _():
            copy(hist.at[0], hist.at[0], TIME_FWD, sibling).wait_recv()

        @pl.when(c == 1)
        def _():
            copy(hist.at[2], hist.at[2], TIME_FWD, sibling).wait_recv()

    @pl.when((c == 0) & (zl > 1))
    def _():
        copy(hist.at[2], hist.at[2], TIME_RELAY, sibling).wait_recv()

    for j in range(3):

        @pl.when(f > j)
        def _(j=j):
            normalize(3 + j, hist.at[j])

        @pl.when(f <= j)
        def _(j=j):
            xn[3 + j] = jnp.zeros((ROWS, D), bf16)

    for s in theirs:
        s.step4()
    for s in theirs:
        s.step5()
    for s in streams:
        s.finish()
    copy(own, own, W_Z, sibling).wait_send()

    r_i = lax.broadcasted_iota(jnp.int32, (256, 256), 0) // 64
    c_i = lax.broadcasted_iota(jnp.int32, (256, 256), 1) // 64
    bd = jnp.where(r_i == c_i, 1.0, 0.0).astype(bf16)

    def weights(p, lo, hi):
        w = G[p, :, :, :, 0:QKV, :].reshape(32 * QKV, D)
        return w[lo:hi]

    x0 = xn[0]
    tp = nt_dot(x0, weights(1, 0, 3 * D))
    tq = unit(tp[:, 0:D], bd).astype(f32)
    head_of = lax.broadcasted_iota(jnp.int32, (1, D), 1) // 64
    ct = jnp.zeros((1, D), f32)
    for h in range(HEADS):
        ct = jnp.where(head_of == h, temper[1, h] * 0.125, ct)
    scores, values = [], []
    for j in range(4):
        if j == 0:
            kv = tp[:, D:]
        else:
            kv = nt_dot(xn[2 + j], weights(1, D, 3 * D))
        k = unit(kv[:, 0:D], bd).astype(f32)
        s = head_sums_all(tq * k, bd) * ct
        if j > 0:
            s = s + jnp.where(f >= j, 0.0, BIG)
        scores.append(s)
        values.append(kv[:, D:].astype(bf16).astype(f32))
    top = jnp.maximum(
        jnp.maximum(scores[0], scores[1]), jnp.maximum(scores[2], scores[3])
    )
    es = [jnp.exp(s - top) for s in scores]
    inv = 1.0 / (es[0] + es[1] + es[2] + es[3])
    acc = jnp.zeros((ROWS, D), f32)
    for e, v in zip(es, values):
        acc = acc + (e * inv).astype(bf16).astype(f32) * v
    time_mix = acc.astype(bf16)

    sp = nt_dot(x0, weights(0, 0, 3 * D))
    sq = unit(sp[:, 0:D], bd)
    ones = jnp.ones((3 * ROWS, 128), bf16)

    def put(i, kv):
        kbuf[i * ROWS : (i + 1) * ROWS, :] = unit(kv[:, 0:D], bd)
        v = kv[:, D:].astype(bf16)
        for t in range(4):
            vext[i * ROWS : (i + 1) * ROWS, 256 * t : 256 * t + 128] = v[
                :, 128 * t : 128 * t + 128
            ]

    for t in range(4):
        vext[:, 256 * t + 128 : 256 * t + 256] = ones
    put(0, sp[:, D:])

    @pl.when(has_up)
    def _():
        copy(state, lat.at[0], LAT_DOWN, sibling).wait_recv()
        normalize(1, lat.at[0])

    @pl.when(has_down)
    def _():
        copy(state, lat.at[1], LAT_UP, sibling).wait_recv()
        normalize(2, lat.at[1])

    pl.when(jnp.logical_not(has_up))(
        lambda: xn.at[1].__setitem__(Ellipsis, jnp.zeros((ROWS, D), bf16))
    )
    pl.when(jnp.logical_not(has_down))(
        lambda: xn.at[2].__setitem__(Ellipsis, jnp.zeros((ROWS, D), bf16))
    )
    for i in (1, 2):
        put(i, nt_dot(xn[i], weights(0, D, 3 * D)))

    lane = lax.broadcasted_iota(jnp.int32, (ROWS, 128), 1)
    mixes = []
    for t in range(4):
        q = sq[:, 128 * t : 128 * t + 128]
        k = kbuf[:, 128 * t : 128 * t + 128]
        halves = []
        for e in range(2):
            qe = jnp.where((lane < 64) == (e == 0), q, jnp.zeros_like(q))
            parts = []
            for i in range(3):
                parts.append(nt_dot(qe, k[i * ROWS : (i + 1) * ROWS]) + bias[i])
            top = jnp.maximum(
                jnp.maximum(
                    jnp.max(parts[0], axis=1, keepdims=True),
                    jnp.max(parts[1], axis=1, keepdims=True),
                ),
                jnp.max(parts[2], axis=1, keepdims=True),
            )
            cs = temper[0, 2 * t + e] * 0.125
            o = jnp.zeros((ROWS, 256), f32)
            for i in range(3):
                p = jnp.exp((parts[i] - top) * cs).astype(bf16)
                o = o + jnp.dot(
                    p,
                    vext[i * ROWS : (i + 1) * ROWS, 256 * t : 256 * t + 256],
                    preferred_element_type=f32,
                )
            halves.append(o[:, 0:128] / o[:, 128:256])
        mixes.append(jnp.where(lane < 64, halves[0], halves[1]).astype(bf16))
    space_mix = jnp.concatenate(mixes, axis=1)

    fs = G[0, :, :, :, QKV:SHARD, :].reshape(D, D)
    ft = G[1, :, :, :, QKV:SHARD, :].reshape(D, D)
    update = (nt_dot(space_mix, fs) + nt_dot(time_mix, ft))[0:LON]
    lv = jnp.full((1, D), level[0], jnp.int32).astype(f32)
    step = math.log(20.0) / 16
    s0 = 0.1 * jnp.exp((lv + 1.0) * step)
    s1 = 0.1 * jnp.exp(lv * step)
    var = 1.0 + s0 * s0
    st = state[...].astype(f32)
    nz = noise[...].astype(f32)
    denoised = st * (1.0 / var) + (s0 * lax.rsqrt(var)) * update
    stepped = denoised + s1 * ((0.8 / s0) * (st - denoised) + 0.6 * nz)
    out[...] = jnp.where(lv == 0.0, 2.0 * nz, stepped).astype(bf16)

    pl.when(has_down)(lat_to_down.wait_send)
    pl.when(has_up)(lat_to_up.wait_send)
    pl.when(has_next)(time_z.wait_send)
    pl.when(c == 0)(time_sib.wait_send)

    @pl.when(has_prev)
    def _():
        copy(hist.at[1], hist.at[0], TIME_FWD, sibling).wait_send()

        @pl.when(relays)
        def _():
            copy(hist.at[1], hist.at[2], TIME_RELAY, relay_to).wait_send()


def body(
    noisy,
    perturbation,
    level,
    starts,
    tally,
    gain,
    temper,
    local_w,
    time_w,
    final_w,
):
    smem = pl.BlockSpec(memory_space=pltpu.SMEM)
    vmem = pl.BlockSpec(memory_space=pltpu.VMEM)
    out = pl.pallas_call(
        kernel,
        out_shape=jax.ShapeDtypeStruct((LON, D), bf16),
        in_specs=[smem] * 4 + [vmem] * 6,
        out_specs=vmem,
        scratch_shapes=[
            pltpu.VMEM((2, 4, 2, 4, SHARD, D), bf16),
            pltpu.VMEM((3, LON, D), bf16),
            pltpu.VMEM((2, LON, D), bf16),
            pltpu.VMEM((6, ROWS, D), bf16),
            pltpu.VMEM((3 * ROWS, D), bf16),
            pltpu.VMEM((3 * ROWS, 2 * D), bf16),
            pltpu.VMEM((3, ROWS, ROWS), f32),
            pltpu.SemaphoreType.DMA((SLOTS,)),
            pltpu.SemaphoreType.DMA((SLOTS,)),
        ],
        compiler_params=pltpu.CompilerParams(
            collective_id=0, has_side_effects=True, vmem_limit_bytes=56 * 1024 * 1024
        ),
        name="step",
    )(
        level,
        starts,
        tally,
        temper,
        noisy.reshape(LON, D),
        perturbation.reshape(LON, D),
        gain.reshape(1, D),
        local_w,
        time_w,
        final_w,
    )
    return out.reshape(noisy.shape)


def solution(mesh):
    return jax.shard_map(
        body,
        mesh=mesh,
        in_specs=(
            P("frame", "band", None, None),
            P("frame", "band", None, None),
            P("frame"),
            P("frame"),
            P(),
            P(),
            P(),
            P(None, "band"),
            P(None, "band"),
            P(None, "band"),
        ),
        out_specs=P("frame", "band", None, None),
        check_vma=False,
    )
```

```python
import math

import jax
import jax.numpy as jnp
from jax import lax
from jax.experimental import pallas as pl
from jax.experimental.pallas import tpu as pltpu
from jax.sharding import PartitionSpec as P

MESH = pl.DeviceIdType.MESH
HEADS = 8
LON = 180
WINDOW = 60
ROWS = 192
D = 512
SHARD = 64
QKV = 48
BIG = -1e30
epsilon = 1e-06
f32 = jnp.float32
bf16 = jnp.bfloat16

LAT_UP, LAT_DOWN, TIME_Z, TIME_SIB, TIME_FWD, TIME_RELAY = range(6)
EDGE = 6
LATB, HOP = 14, 15
STREAM0 = 16
PER_STREAM = 20
SLOTS = STREAM0 + 4 * PER_STREAM


def nt_dot(a, b):
    return lax.dot_general(a, b, (((1,), (1,)), ((), ())), preferred_element_type=f32)


def head_sums(x, bd):
    hi = x.astype(bf16)
    lo = (x - hi.astype(f32)).astype(bf16)
    return jnp.dot(hi, bd, preferred_element_type=f32) + jnp.dot(
        lo, bd, preferred_element_type=f32
    )


def head_sums_all(x, bd):
    return jnp.concatenate(
        [head_sums(x[:, 256 * i : 256 * i + 256], bd) for i in range(2)], axis=1
    )


def unit(u, bd):
    mean = head_sums_all(u * u, bd) * (1.0 / 64)
    return (u * lax.rsqrt(mean + epsilon)).astype(bf16)


def coords():
    f = lax.axis_index("frame")
    b = lax.axis_index("band")
    return f, b, f // 2, f % 2, b // 8, (b // 4) % 2, b % 4


def kernel(
    level,
    starts,
    tally,
    temper,
    state,
    noise,
    gain,
    local_w,
    time_w,
    final_w,
    out,
    G,
    hist,
    lat,
    xn,
    kbuf,
    vext,
    bias,
    hop,
    mix,
    ssem,
    rsem,
    lsem,
    ready,
):
    f, b, zl, c, y, zh, x = coords()
    oc = 1 - c

    def own_copies(p, w):
        return (
            pltpu.make_async_copy(w, G.at[p, y, zh, x, pl.ds(0, QKV), :], lsem.at[0]),
            pltpu.make_async_copy(
                final_w.at[:, pl.ds(p * D, D)],
                G.at[p, y, zh, x, pl.ds(QKV, SHARD - QKV), :],
                lsem.at[1],
            ),
        )

    for p, w in enumerate((local_w, time_w)):

        @pl.when(c == p)
        def _(p=p, w=w):
            for d in own_copies(p, w):
                d.start()

    def at(dx=0, dy=0, dzl=0, cc=None, zhh=None):
        yy = (y + dy + 4) % 4
        xx = (x + dx + 4) % 4
        z2 = zh if zhh is None else zhh
        c2 = c if cc is None else cc
        return {"frame": (zl + dzl) * 2 + c2, "band": (yy * 2 + z2) * 4 + xx}

    sibling = at(cc=oc)
    xr, xl, yr, yl = at(dx=1), at(dx=-1), at(dy=1), at(dy=-1)
    x2, y2 = at(dx=2), at(dy=2)

    def over_z(zz):
        return {"frame": zz * 2 + c, "band": (y * 2 + 1 - zh) * 4 + x}

    source = over_z(jnp.where(zl < 4, 7, 0))
    targets = [over_z(jnp.where(zl == 0, 7 - i, i)) for i in range(4)]
    z_next, z_prev = at(dzl=1), at(dzl=-1)
    relay_to, relay_from = at(dzl=1, cc=0), at(dzl=-1, cc=1)
    up = {"frame": f, "band": b - 1}
    down = {"frame": f, "band": b + 1}

    has_prev, has_next = zl > 0, zl < 7
    has_up, has_down = b > 0, b < 31
    relays = (c == 1) & has_next
    relayed = (c == 0) & has_prev

    barrier = pltpu.get_barrier_semaphore()

    def greet(dev):
        pl.semaphore_signal(barrier, inc=1, device_id=dev, device_id_type=MESH)

    is_edge = (zl == 0) | (zl == 7)
    cross_up, cross_down = (x == 0) & has_up, (x == 3) & has_down
    late = zh == 1
    for dev in (sibling, xr, xl, yr, yl, x2, y2):
        greet(dev)
    count = 7
    for cond, dev in (
        (has_next, z_next),
        (has_prev, z_prev),
        (relays, relay_to),
        (relayed, relay_from),
    ):
        pl.when(cond)(lambda dev=dev: greet(dev))
        count = count + jnp.where(cond, 1, 0)
    cross = [(zh >= 0, source)] + [(is_edge, dev) for dev in targets]
    up2 = {"frame": f, "band": b - 2}
    down2 = {"frame": f, "band": b + 2}
    relay_up, relay_down = (x == 1) & (b > 1), (x == 2) & (b < 30)
    rows_from = [
        (cross_up, up),
        (cross_down, down),
        (cross_up, up2),
        (cross_down, down2),
    ]
    cross += rows_from + [(relay_up, up2), (relay_down, down2)]
    for cond, dev in cross:
        pl.when(cond & (zh == 0))(lambda dev=dev: greet(dev))
        count = count + jnp.where(cond & late, 1, 0)
    pl.semaphore_wait(barrier, count)
    for i, cond, dev in [(0, zh >= 0, source)] + [(1,) + r for r in rows_from]:

        @pl.when(cond & late)
        def _(i=i, dev=dev):
            pl.semaphore_signal(
                ready.at[i], inc=1, device_id=dev, device_id_type=MESH
            )

    for p, w in enumerate((local_w, time_w)):

        @pl.when(c == p)
        def _(p=p, w=w):
            for d in own_copies(p, w):
                d.wait()


    def copy(src, dst, slot, dev):
        return pltpu.make_async_remote_copy(
            src_ref=src,
            dst_ref=dst,
            send_sem=ssem.at[slot],
            recv_sem=rsem.at[slot],
            device_id=dev,
            device_id_type=MESH,
        )

    def gref(cc, yy, zz, xx, r0, r1):
        return G.at[cc, yy, zz, xx, pl.ds(r0, r1 - r0), :]

    lat_to_down = copy(state, lat.at[0], LAT_DOWN, down)
    lat_to_up = copy(state, lat.at[1], LAT_UP, up)
    time_z = copy(state, hist.at[1], TIME_Z, z_next)
    time_sib = copy(state, hist.at[0], TIME_SIB, sibling)

    def block(zz, i):
        return gref(c, y, zz, x, 32 * i, 32 * i + 32)

    def edge_copy(i, j):
        return pltpu.make_async_remote_copy(
            src_ref=block(zh, i),
            dst_ref=block(zh, i),
            send_sem=ssem.at[EDGE + 2 * j + i],
            recv_sem=rsem.at[EDGE + i],
            device_id=targets[j],
            device_id_type=MESH,
        )

    edges = [edge_copy(i, j) for j in range(4) for i in range(2)]

    def send_edges():
        for e in edges:
            e.start()

    pl.when(late & is_edge)(send_edges)

    fa, fb = pl.ds(0, D // 2), pl.ds(D // 2, D // 2)
    plain_down, plain_up = has_down & (x < 3), has_up & (x > 0)
    a_down = copy(state.at[:, fa], lat.at[0, :, fa], LAT_DOWN, down)
    a_up = copy(state.at[:, fa], lat.at[1, :, fa], LAT_UP, up)
    hop_down = copy(state.at[:, fb], hop, HOP, xl)
    hop_up = copy(state.at[:, fb], hop, HOP, xr)
    b_down = copy(hop, lat.at[0, :, fb], LATB, down2)
    b_up = copy(hop, lat.at[1, :, fb], LATB, up2)
    hop_in = relay_down | relay_up
    pl.when(cross_down)(hop_down.start)
    pl.when(cross_up)(hop_up.start)

    def start_cross():
        pl.when(cross_down)(a_down.start)
        pl.when(cross_up)(a_up.start)
        pl.when(relay_down)(b_down.start)
        pl.when(relay_up)(b_up.start)

    class Stream:
        def __init__(self, index, zz, order):
            self.s = STREAM0 + PER_STREAM * index
            self.zz, self.order = zz, order
            self.r0, self.r1 = (0, 32) if order == 0 else (32, 64)
            self.first = (xr, xl, x2) if order == 0 else (yr, yl, y2)
            self.second = (yr, yl, y2) if order == 0 else (xr, xl, x2)

        def at(self, d1, d2):
            dx, dy = (d1, d2) if self.order == 0 else (d2, d1)
            return gref(c, (y + dy + 4) % 4, self.zz, (x + dx + 4) % 4, self.r0, self.r1)

        def line(self, d2, cc):
            rows = pl.ds(self.r0, self.r1 - self.r0)
            if self.order == 0:
                return G.at[cc, (y + d2 + 4) % 4, self.zz, :, rows, :]
            return G.at[cc, :, self.zz, (x + d2 + 4) % 4, rows, :]

        def go(self, ref, slot, dev):
            copy(ref, ref, self.s + slot, dev).start()

        def got(self, ref, slot):
            copy(ref, ref, self.s + slot, sibling).wait_recv()

        def sent(self, ref, slot):
            copy(ref, ref, self.s + slot, sibling).wait_send()

        def spread(self, k, d1):
            for j in range(3):
                self.go(self.at(d1, 0), 3 + 3 * k + j, self.second[j])

        def step1(self):
            for j in range(3):
                self.go(self.at(0, 0), j, self.first[j])
            self.spread(0, 0)

        def step2(self):
            for j, d in enumerate((-1, 1, 2)):
                self.got(self.at(d, 0), j)
                self.spread(j + 1, d)
            self.go(self.line(0, c), 15, sibling)

        def step3(self):
            for j, d2 in enumerate((-1, 1, 2)):
                for k, d1 in enumerate((0, -1, 1, 2)):
                    self.got(self.at(d1, d2), 3 + 3 * k + j)
                self.go(self.line(d2, c), 16 + j, sibling)

        def arrive(self):
            for i, d in enumerate((0, -1, 1, 2)):
                self.got(self.line(d, oc), 15 + i)

        def finish(self):
            for i in range(15):
                self.sent(self.at(0, 0), i)
            for i in range(4):
                self.sent(self.line(i, c), 15 + i)

    streams = [
        Stream(0, zh, 0),
        Stream(1, zh, 1),
        Stream(2, 1 - zh, 0),
        Stream(3, 1 - zh, 1),
    ]
    mine, theirs = streams[:2], streams[2:]
    for s in mine:
        s.step1()

    def normalize(i, row_ref):
        s = row_ref[...].astype(f32)
        r = lax.rsqrt(jnp.mean(s * s, axis=-1, keepdims=True) + epsilon)
        xn[i, 0:LON, :] = (s * r * gain[...]).astype(bf16)
        xn[i, LON:ROWS, :] = jnp.zeros((ROWS - LON, D), bf16)

    normalize(0, state)

    for s in mine:
        s.step2()
    pl.when(hop_in)(hop_down.wait_recv)
    pl.when(late)(start_cross)
    pl.when(plain_down)(lat_to_down.start)
    pl.when(plain_up)(lat_to_up.start)
    pl.when(has_next)(time_z.start)
    pl.when(c == 0)(time_sib.start)

    shift = starts[...]
    qi = lax.broadcasted_iota(jnp.int32, (ROWS, ROWS), 0)
    ki = lax.broadcasted_iota(jnp.int32, (ROWS, ROWS), 1)

    def window(i):
        d = i - shift
        d = jnp.where(d < 0, d + LON, d)
        return jnp.where(d >= WINDOW, 1, 0) + jnp.where(d >= 2 * WINDOW, 1, 0)

    same = window(qi) == window(ki)
    n_above = jnp.where(has_up, tally[jnp.maximum(b - 1, 0)], 0)
    n_below = jnp.where(has_down, tally[jnp.minimum(b + 1, 31)], 0)
    n_own = tally[b]
    for i, n in enumerate((n_own, n_above, n_below)):
        seen = same & (ki < n)
        if i == 0:
            seen = seen | (qi == ki)
        bias[i] = jnp.where(seen, 0.0, BIG)

    @pl.when((zh == 0) & is_edge)
    def _():
        pl.semaphore_wait(ready.at[0], 4)
        send_edges()

    for i, s in enumerate(theirs):
        copy(block(1 - zh, i), block(1 - zh, i), EDGE + i, sibling).wait_recv()
        s.step1()

    @pl.when(has_prev)
    def _():
        copy(state, hist.at[1], TIME_Z, sibling).wait_recv()

        @pl.when(c == 1)
        def _():
            copy(hist.at[1], hist.at[0], TIME_FWD, sibling).start()

        @pl.when(c == 0)
        def _():
            copy(hist.at[1], hist.at[2], TIME_FWD, sibling).start()

        @pl.when(relays)
        def _():
            copy(hist.at[1], hist.at[2], TIME_RELAY, relay_to).start()

    @pl.when((zh == 0) & (cross_up | cross_down | hop_in))
    def _():
        pl.semaphore_wait(ready.at[1], 1)
        start_cross()

    for s in mine:
        s.step3()
    for s in theirs:
        s.step2()

    @pl.when(c == 1)
    def _():
        copy(state, hist.at[0], TIME_SIB, sibling).wait_recv()

    @pl.when(has_prev)
    def _():
        @pl.when(c == 0)
        def _():
            copy(hist.at[0], hist.at[0], TIME_FWD, sibling).wait_recv()

        @pl.when(c == 1)
        def _():
            copy(hist.at[2], hist.at[2], TIME_FWD, sibling).wait_recv()

    @pl.when((c == 0) & (zl > 1))
    def _():
        copy(hist.at[2], hist.at[2], TIME_RELAY, sibling).wait_recv()

    for j in range(3):

        @pl.when(f > j)
        def _(j=j):
            normalize(3 + j, hist.at[j])

        @pl.when(f <= j)
        def _(j=j):
            xn[3 + j] = jnp.zeros((ROWS, D), bf16)

    for s in theirs:
        s.step3()
    r_i = lax.broadcasted_iota(jnp.int32, (256, 256), 0) // 64
    c_i = lax.broadcasted_iota(jnp.int32, (256, 256), 1) // 64
    bd = jnp.where(r_i == c_i, 1.0, 0.0).astype(bf16)

    def weights(p, lo, hi):
        w = G[p, :, :, :, 0:QKV, :].reshape(32 * QKV, D)
        return w[lo:hi]

    def temporal():
        x0 = xn[0]
        tp = nt_dot(x0, weights(1, 0, 3 * D))
        tq = unit(tp[:, 0:D], bd).astype(f32)
        head_of = lax.broadcasted_iota(jnp.int32, (1, D), 1) // 64
        ct = jnp.zeros((1, D), f32)
        for h in range(HEADS):
            ct = jnp.where(head_of == h, temper[1, h] * 0.125, ct)
        scores, values = [], []
        for j in range(4):
            if j == 0:
                kv = tp[:, D:]
            else:
                kv = nt_dot(xn[2 + j], weights(1, D, 3 * D))
            k = unit(kv[:, 0:D], bd).astype(f32)
            s = head_sums_all(tq * k, bd) * ct
            if j > 0:
                s = s + jnp.where(f >= j, 0.0, BIG)
            scores.append(s)
            values.append(kv[:, D:].astype(bf16).astype(f32))
        top = jnp.maximum(
            jnp.maximum(scores[0], scores[1]), jnp.maximum(scores[2], scores[3])
        )
        es = [jnp.exp(s - top) for s in scores]
        inv = 1.0 / (es[0] + es[1] + es[2] + es[3])
        acc = jnp.zeros((ROWS, D), f32)
        for e, v in zip(es, values):
            acc = acc + (e * inv).astype(bf16).astype(f32) * v
        mix[1] = acc.astype(bf16)

    def windows():
        x0 = xn[0]
        sp = nt_dot(x0, weights(0, 0, 3 * D))
        sq = unit(sp[:, 0:D], bd)
        ones = jnp.ones((3 * ROWS, 128), bf16)

        def put(i, kv):
            kbuf[i * ROWS : (i + 1) * ROWS, :] = unit(kv[:, 0:D], bd)
            v = kv[:, D:].astype(bf16)
            for t in range(4):
                vext[i * ROWS : (i + 1) * ROWS, 256 * t : 256 * t + 128] = v[
                    :, 128 * t : 128 * t + 128
                ]

        for t in range(4):
            vext[:, 256 * t + 128 : 256 * t + 256] = ones
        put(0, sp[:, D:])

        @pl.when(plain_up)
        def _():
            copy(state, lat.at[0], LAT_DOWN, sibling).wait_recv()

        @pl.when(plain_down)
        def _():
            copy(state, lat.at[1], LAT_UP, sibling).wait_recv()

        @pl.when(cross_up)
        def _():
            copy(state.at[:, fa], lat.at[0, :, fa], LAT_DOWN, sibling).wait_recv()
            copy(state.at[:, fb], lat.at[0, :, fb], LATB, sibling).wait_recv()

        @pl.when(cross_down)
        def _():
            copy(state.at[:, fa], lat.at[1, :, fa], LAT_UP, sibling).wait_recv()
            copy(state.at[:, fb], lat.at[1, :, fb], LATB, sibling).wait_recv()

        pl.when(has_up)(lambda: normalize(1, lat.at[0]))
        pl.when(has_down)(lambda: normalize(2, lat.at[1]))
        pl.when(jnp.logical_not(has_up))(
            lambda: xn.at[1].__setitem__(Ellipsis, jnp.zeros((ROWS, D), bf16))
        )
        pl.when(jnp.logical_not(has_down))(
            lambda: xn.at[2].__setitem__(Ellipsis, jnp.zeros((ROWS, D), bf16))
        )
        for i in (1, 2):
            put(i, nt_dot(xn[i], weights(0, D, 3 * D)))

        lane = lax.broadcasted_iota(jnp.int32, (ROWS, 128), 1)
        for t in range(4):
            q = sq[:, 128 * t : 128 * t + 128]
            k = kbuf[:, 128 * t : 128 * t + 128]
            halves = []
            for e in range(2):
                qe = jnp.where((lane < 64) == (e == 0), q, jnp.zeros_like(q))
                parts = []
                for i in range(3):
                    parts.append(nt_dot(qe, k[i * ROWS : (i + 1) * ROWS]) + bias[i])
                top = jnp.maximum(
                    jnp.maximum(
                        jnp.max(parts[0], axis=1, keepdims=True),
                        jnp.max(parts[1], axis=1, keepdims=True),
                    ),
                    jnp.max(parts[2], axis=1, keepdims=True),
                )
                cs = temper[0, 2 * t + e] * 0.125
                o = jnp.zeros((ROWS, 256), f32)
                for i in range(3):
                    p = jnp.exp((parts[i] - top) * cs).astype(bf16)
                    o = o + jnp.dot(
                        p,
                        vext[i * ROWS : (i + 1) * ROWS, 256 * t : 256 * t + 256],
                        preferred_element_type=f32,
                    )
                halves.append(o[:, 0:128] / o[:, 128:256])
            mix[0, :, 128 * t : 128 * t + 128] = jnp.where(
                lane < 64, halves[0], halves[1]
            ).astype(bf16)

    def attention(i, carry):
        @pl.when(i == 1)
        def _():
            for s in streams:
                s.arrive()

        pl.when((i + c) % 2 == 0)(windows)
        pl.when((i + c) % 2 == 1)(temporal)
        return carry

    lax.fori_loop(0, 2, attention, 0)

    fs = G[0, :, :, :, QKV:SHARD, :].reshape(D, D)
    ft = G[1, :, :, :, QKV:SHARD, :].reshape(D, D)
    update = (nt_dot(mix[0], fs) + nt_dot(mix[1], ft))[0:LON]
    lv = jnp.broadcast_to(level[...], (1, D)).astype(f32)
    step = math.log(20.0) / 16
    s0 = 0.1 * jnp.exp((lv + 1.0) * step)
    s1 = 0.1 * jnp.exp(lv * step)
    var = 1.0 + s0 * s0
    st = state[...].astype(f32)
    nz = noise[...].astype(f32)
    denoised = st * (1.0 / var) + (s0 * lax.rsqrt(var)) * update
    stepped = denoised + s1 * ((0.8 / s0) * (st - denoised) + 0.6 * nz)
    out[...] = jnp.where(lv == 0.0, 2.0 * nz, stepped).astype(bf16)

    for stream in streams:
        stream.finish()

    @pl.when(is_edge)
    def _():
        for e in edges:
            e.wait_send()

    pl.when(plain_down)(lat_to_down.wait_send)
    pl.when(plain_up)(lat_to_up.wait_send)

    @pl.when(cross_down)
    def _():
        hop_down.wait_send()
        a_down.wait_send()

    @pl.when(cross_up)
    def _():
        hop_up.wait_send()
        a_up.wait_send()

    pl.when(hop_in)(b_down.wait_send)
    pl.when(has_next)(time_z.wait_send)
    pl.when(c == 0)(time_sib.wait_send)

    @pl.when(has_prev)
    def _():
        copy(hist.at[1], hist.at[0], TIME_FWD, sibling).wait_send()

        @pl.when(relays)
        def _():
            copy(hist.at[1], hist.at[2], TIME_RELAY, relay_to).wait_send()


def body(
    noisy,
    perturbation,
    level,
    starts,
    tally,
    gain,
    temper,
    local_w,
    time_w,
    final_w,
):
    smem = pl.BlockSpec(memory_space=pltpu.SMEM)
    vmem = pl.BlockSpec(memory_space=pltpu.VMEM)
    out = pl.pallas_call(
        kernel,
        out_shape=jax.ShapeDtypeStruct((LON, D), bf16),
        in_specs=[vmem] * 2 + [smem] * 2 + [vmem] * 3 + [pl.BlockSpec(memory_space=pl.ANY)] * 3,
        out_specs=vmem,
        scratch_shapes=[
            pltpu.VMEM((2, 4, 2, 4, SHARD, D), bf16),
            pltpu.VMEM((3, LON, D), bf16),
            pltpu.VMEM((2, LON, D), bf16),
            pltpu.VMEM((6, ROWS, D), bf16),
            pltpu.VMEM((3 * ROWS, D), bf16),
            pltpu.VMEM((3 * ROWS, 2 * D), bf16),
            pltpu.VMEM((3, ROWS, ROWS), f32),
            pltpu.VMEM((LON, D // 2), bf16),
            pltpu.VMEM((2, ROWS, D), bf16),
            pltpu.SemaphoreType.DMA((SLOTS,)),
            pltpu.SemaphoreType.DMA((SLOTS,)),
            pltpu.SemaphoreType.DMA((2,)),
            pltpu.SemaphoreType.REGULAR((2,)),
        ],
        compiler_params=pltpu.CompilerParams(
            collective_id=0, has_side_effects=True, vmem_limit_bytes=56 * 1024 * 1024
        ),
        name="step",
    )(
        level.reshape(1, 1),
        starts.reshape(1, 1),
        tally,
        temper,
        noisy.reshape(LON, D),
        perturbation.reshape(LON, D),
        gain.reshape(1, D),
        local_w.T,
        time_w.T,
        final_w.T,
    )
    return out.reshape(noisy.shape)


def solution(mesh):
    return jax.shard_map(
        body,
        mesh=mesh,
        in_specs=(
            P("frame", "band", None, None),
            P("frame", "band", None, None),
            P("frame"),
            P("frame"),
            P(),
            P(),
            P(),
            P(None, "band"),
            P(None, "band"),
            P(None, "band"),
        ),
        out_specs=P("frame", "band", None, None),
        check_vma=False,
    )
```

```python
import math

import jax
import jax.numpy as jnp
from jax import lax
from jax.experimental import pallas as pl
from jax.experimental.pallas import tpu as pltpu
from jax.sharding import PartitionSpec as P

MESH = pl.DeviceIdType.MESH
HEADS = 8
LON = 180
WINDOW = 60
ROWS = 192
D = 512
SHARD = 64
QKV = 48
BIG = -1e30
epsilon = 1e-06
f32 = jnp.float32
bf16 = jnp.bfloat16

LAT_UP, LAT_DOWN, LATB, HOP, TIME_Z, TIME_SIB, TIME_FWD, TIME_RELAY = range(8)
EDGE = 8
NEAR = 2
STREAM0 = EDGE + 2 * (8 - NEAR)
PER_STREAM = 20
SLOTS = STREAM0 + 4 * PER_STREAM


def nt_dot(a, b):
    return lax.dot_general(a, b, (((1,), (1,)), ((), ())), preferred_element_type=f32)


def head_sums(x, bd):
    hi = x.astype(bf16)
    lo = (x - hi.astype(f32)).astype(bf16)
    return jnp.dot(hi, bd, preferred_element_type=f32) + jnp.dot(
        lo, bd, preferred_element_type=f32
    )


def head_sums_all(x, bd):
    return jnp.concatenate(
        [head_sums(x[:, 256 * i : 256 * i + 256], bd) for i in range(2)], axis=1
    )


def unit(u, bd):
    mean = head_sums_all(u * u, bd) * (1.0 / 64)
    return (u * lax.rsqrt(mean + epsilon)).astype(bf16)


def coords():
    f = lax.axis_index("frame")
    b = lax.axis_index("band")
    return f, b, f // 2, f % 2, b // 8, (b // 4) % 2, b % 4


def kernel(
    level,
    starts,
    tally,
    temper,
    state_in,
    noise_in,
    gain,
    local_w,
    time_w,
    final_w,
    out,
    G,
    hist,
    lat,
    xn,
    kbuf,
    vext,
    bias,
    hop,
    mix,
    state,
    noise,
    ssem,
    rsem,
    lsem,
    ready,
):
    f, b, zl, c, y, zh, x = coords()
    oc = 1 - c

    def own_copies(p, w):
        return (
            pltpu.make_async_copy(w, G.at[p, y, zh, x, pl.ds(0, QKV), :], lsem.at[0]),
            pltpu.make_async_copy(
                final_w.at[:, pl.ds(p * D, D)],
                G.at[p, y, zh, x, pl.ds(QKV, SHARD - QKV), :],
                lsem.at[1],
            ),
        )

    load_state = pltpu.make_async_copy(state_in, state, lsem.at[2])
    load_noise = pltpu.make_async_copy(noise_in, noise, lsem.at[3])
    load_state.start()
    for p, w in enumerate((local_w, time_w)):

        @pl.when(c == p)
        def _(p=p, w=w):
            for d in own_copies(p, w):
                d.start()

    def at(dx=0, dy=0, dzl=0, cc=None, zhh=None):
        yy = (y + dy + 4) % 4
        xx = (x + dx + 4) % 4
        z2 = zh if zhh is None else zhh
        c2 = c if cc is None else cc
        return {"frame": (zl + dzl) * 2 + c2, "band": (yy * 2 + z2) * 4 + xx}

    sibling = at(cc=oc)
    xr, xl, yr, yl = at(dx=1), at(dx=-1), at(dy=1), at(dy=-1)
    x2, y2 = at(dx=2), at(dy=2)

    def over_z(zz):
        return {"frame": zz * 2 + c, "band": (y * 2 + 1 - zh) * 4 + x}

    near = jnp.where(zh == 0, NEAR, 4)
    source = over_z(jnp.where(zl < near, 7, 0))
    first = jnp.where(zl == 0, jnp.where(zh == 0, 4, NEAR), 0)
    wide = jnp.where(zh == 0, 4, jnp.where(zl == 0, 8 - NEAR, NEAR))
    targets = [over_z((first + i) % 8) for i in range(8 - NEAR)]
    z_next, z_prev = at(dzl=1), at(dzl=-1)
    relay_to, relay_from = at(dzl=1, cc=0), at(dzl=-1, cc=1)
    up = {"frame": f, "band": b - 1}
    down = {"frame": f, "band": b + 1}

    has_prev, has_next = zl > 0, zl < 7
    has_up, has_down = b > 0, b < 31
    relays = (c == 1) & has_next
    relayed = (c == 0) & has_prev

    barrier = pltpu.get_barrier_semaphore()

    def greet(dev):
        pl.semaphore_signal(barrier, inc=1, device_id=dev, device_id_type=MESH)

    is_edge = (zl == 0) | (zl == 7)
    cross_up, cross_down = (x == 0) & has_up, (x == 3) & has_down
    late = zh == 1
    for dev in (sibling, xr, xl, yr, yl, x2, y2):
        greet(dev)
    count = 7
    for cond, dev in (
        (has_next, z_next),
        (has_prev, z_prev),
        (relays, relay_to),
        (relayed, relay_from),
    ):
        pl.when(cond)(lambda dev=dev: greet(dev))
        count = count + jnp.where(cond, 1, 0)
    cross = [(zh >= 0, source)]
    cross += [(is_edge & (i < wide), dev) for i, dev in enumerate(targets)]
    up2 = {"frame": f, "band": b - 2}
    down2 = {"frame": f, "band": b + 2}
    relay_up, relay_down = (x == 1) & (b > 1), (x == 2) & (b < 30)
    rows_from = [
        (cross_up, up),
        (cross_down, down),
        (cross_up, up2),
        (cross_down, down2),
    ]
    cross += rows_from + [(relay_up, up2), (relay_down, down2)]
    for cond, dev in cross:
        pl.when(cond & (zh == 0))(lambda dev=dev: greet(dev))
        count = count + jnp.where(cond & late, 1, 0)
    load_noise.start()
    load_state.wait()
    pl.semaphore_wait(barrier, count)
    for i, cond, dev in [(0, zh >= 0, source)] + [(1,) + r for r in rows_from]:

        @pl.when(cond & late)
        def _(i=i, dev=dev):
            pl.semaphore_signal(
                ready.at[i], inc=1, device_id=dev, device_id_type=MESH
            )

    for p, w in enumerate((local_w, time_w)):

        @pl.when(c == p)
        def _(p=p, w=w):
            for d in own_copies(p, w):
                d.wait()


    def copy(src, dst, slot, dev):
        return pltpu.make_async_remote_copy(
            src_ref=src,
            dst_ref=dst,
            send_sem=ssem.at[slot],
            recv_sem=rsem.at[slot],
            device_id=dev,
            device_id_type=MESH,
        )

    def gref(cc, yy, zz, xx, r0, r1):
        return G.at[cc, yy, zz, xx, pl.ds(r0, r1 - r0), :]

    lat_to_down = copy(state, lat.at[0], LAT_DOWN, down)
    lat_to_up = copy(state, lat.at[1], LAT_UP, up)
    time_z = copy(state, hist.at[1], TIME_Z, z_next)
    time_sib = copy(state, hist.at[0], TIME_SIB, sibling)

    def block(zz, i):
        return gref(c, y, zz, x, 32 * i, 32 * i + 32)

    def edge_copy(i, j):
        return pltpu.make_async_remote_copy(
            src_ref=block(zh, i),
            dst_ref=block(zh, i),
            send_sem=ssem.at[EDGE + 2 * j + i],
            recv_sem=rsem.at[EDGE + i],
            device_id=targets[j],
            device_id_type=MESH,
        )

    edges = [
        (j < wide, edge_copy(i, j)) for j in range(8 - NEAR) for i in range(2)
    ]

    def send_edges():
        for cond, e in edges:
            pl.when(cond)(e.start)

    pl.when(late & is_edge)(send_edges)

    fa, fb = pl.ds(0, D // 2), pl.ds(D // 2, D // 2)
    plain_down, plain_up = has_down & (x < 3), has_up & (x > 0)
    a_down = copy(state.at[:, fa], lat.at[0, :, fa], LAT_DOWN, down)
    a_up = copy(state.at[:, fa], lat.at[1, :, fa], LAT_UP, up)
    hop_down = copy(state.at[:, fb], hop, HOP, xl)
    hop_up = copy(state.at[:, fb], hop, HOP, xr)
    b_down = copy(hop, lat.at[0, :, fb], LATB, down2)
    b_up = copy(hop, lat.at[1, :, fb], LATB, up2)
    hop_in = relay_down | relay_up
    pl.when(cross_down)(hop_down.start)
    pl.when(cross_up)(hop_up.start)

    def start_cross():
        pl.when(cross_down)(a_down.start)
        pl.when(cross_up)(a_up.start)
        pl.when(relay_down)(b_down.start)
        pl.when(relay_up)(b_up.start)

    class Stream:
        def __init__(self, index, zz, order):
            self.s = STREAM0 + PER_STREAM * index
            self.zz, self.order = zz, order
            self.r0, self.r1 = (0, 32) if order == 0 else (32, 64)
            self.first = (xr, xl, x2) if order == 0 else (yr, yl, y2)
            self.second = (yr, yl, y2) if order == 0 else (xr, xl, x2)

        def at(self, d1, d2):
            dx, dy = (d1, d2) if self.order == 0 else (d2, d1)
            return gref(c, (y + dy + 4) % 4, self.zz, (x + dx + 4) % 4, self.r0, self.r1)

        def line(self, d2, cc):
            rows = pl.ds(self.r0, self.r1 - self.r0)
            if self.order == 0:
                return G.at[cc, (y + d2 + 4) % 4, self.zz, :, rows, :]
            return G.at[cc, :, self.zz, (x + d2 + 4) % 4, rows, :]

        def go(self, ref, slot, dev):
            copy(ref, ref, self.s + slot, dev).start()

        def got(self, ref, slot):
            copy(ref, ref, self.s + slot, sibling).wait_recv()

        def sent(self, ref, slot):
            copy(ref, ref, self.s + slot, sibling).wait_send()

        def spread(self, k, d1):
            for j in range(3):
                self.go(self.at(d1, 0), 3 + 3 * k + j, self.second[j])

        def step1(self):
            for j in range(3):
                self.go(self.at(0, 0), j, self.first[j])
            self.spread(0, 0)

        def step2(self):
            for j, d in enumerate((-1, 1, 2)):
                self.got(self.at(d, 0), j)
                self.spread(j + 1, d)
            self.go(self.line(0, c), 15, sibling)

        def step3(self):
            for j, d2 in enumerate((-1, 1, 2)):
                for k, d1 in enumerate((0, -1, 1, 2)):
                    self.got(self.at(d1, d2), 3 + 3 * k + j)
                self.go(self.line(d2, c), 16 + j, sibling)

        def arrive(self):
            for i, d in enumerate((0, -1, 1, 2)):
                self.got(self.line(d, oc), 15 + i)

        def finish(self):
            for i in range(15):
                self.sent(self.at(0, 0), i)
            for i in range(4):
                self.sent(self.line(i, c), 15 + i)

    streams = [
        Stream(0, zh, 0),
        Stream(1, zh, 1),
        Stream(2, 1 - zh, 0),
        Stream(3, 1 - zh, 1),
    ]
    mine, theirs = streams[:2], streams[2:]
    for s in mine:
        s.step1()

    def normalize(i, row_ref):
        s = row_ref[...].astype(f32)
        r = lax.rsqrt(jnp.mean(s * s, axis=-1, keepdims=True) + epsilon)
        xn[i, 0:LON, :] = (s * r * gain[...]).astype(bf16)
        xn[i, LON:ROWS, :] = jnp.zeros((ROWS - LON, D), bf16)

    normalize(0, state)

    for s in mine:
        s.step2()
    pl.when(hop_in)(hop_down.wait_recv)
    pl.when(late)(start_cross)
    pl.when(plain_down)(lat_to_down.start)
    pl.when(plain_up)(lat_to_up.start)
    pl.when(has_next)(time_z.start)
    pl.when(c == 0)(time_sib.start)

    shift = starts[...]
    qi = lax.broadcasted_iota(jnp.int32, (ROWS, ROWS), 0)
    ki = lax.broadcasted_iota(jnp.int32, (ROWS, ROWS), 1)

    def window(i):
        d = i - shift
        d = jnp.where(d < 0, d + LON, d)
        return jnp.where(d >= WINDOW, 1, 0) + jnp.where(d >= 2 * WINDOW, 1, 0)

    same = window(qi) == window(ki)
    n_above = jnp.where(has_up, tally[jnp.maximum(b - 1, 0)], 0)
    n_below = jnp.where(has_down, tally[jnp.minimum(b + 1, 31)], 0)
    n_own = tally[b]
    for i, n in enumerate((n_own, n_above, n_below)):
        seen = same & (ki < n)
        if i == 0:
            seen = seen | (qi == ki)
        bias[i] = jnp.where(seen, 0.0, BIG)

    @pl.when((zh == 0) & is_edge)
    def _():
        pl.semaphore_wait(ready.at[0], 4)
        send_edges()

    for i, s in enumerate(theirs):
        copy(block(1 - zh, i), block(1 - zh, i), EDGE + i, sibling).wait_recv()
        s.step1()

    @pl.when(has_prev)
    def _():
        copy(state, hist.at[1], TIME_Z, sibling).wait_recv()

        @pl.when(c == 1)
        def _():
            copy(hist.at[1], hist.at[0], TIME_FWD, sibling).start()

        @pl.when(c == 0)
        def _():
            copy(hist.at[1], hist.at[2], TIME_FWD, sibling).start()

        @pl.when(relays)
        def _():
            copy(hist.at[1], hist.at[2], TIME_RELAY, relay_to).start()

    @pl.when((zh == 0) & (cross_up | cross_down | hop_in))
    def _():
        pl.semaphore_wait(ready.at[1], 1)
        start_cross()

    for s in mine:
        s.step3()
    for s in theirs:
        s.step2()

    @pl.when(c == 1)
    def _():
        copy(state, hist.at[0], TIME_SIB, sibling).wait_recv()

    @pl.when(has_prev)
    def _():
        @pl.when(c == 0)
        def _():
            copy(hist.at[0], hist.at[0], TIME_FWD, sibling).wait_recv()

        @pl.when(c == 1)
        def _():
            copy(hist.at[2], hist.at[2], TIME_FWD, sibling).wait_recv()

    @pl.when((c == 0) & (zl > 1))
    def _():
        copy(hist.at[2], hist.at[2], TIME_RELAY, sibling).wait_recv()

    for j in range(3):

        @pl.when(f > j)
        def _(j=j):
            normalize(3 + j, hist.at[j])

        @pl.when(f <= j)
        def _(j=j):
            xn[3 + j] = jnp.zeros((ROWS, D), bf16)

    for s in theirs:
        s.step3()
    r_i = lax.broadcasted_iota(jnp.int32, (256, 256), 0) // 64
    c_i = lax.broadcasted_iota(jnp.int32, (256, 256), 1) // 64
    bd = jnp.where(r_i == c_i, 1.0, 0.0).astype(bf16)

    def weights(p, lo, hi):
        w = G[p, :, :, :, 0:QKV, :].reshape(32 * QKV, D)
        return w[lo:hi]

    def temporal():
        x0 = xn[0]
        tp = nt_dot(x0, weights(1, 0, 3 * D))
        tq = unit(tp[:, 0:D], bd).astype(f32)
        head_of = lax.broadcasted_iota(jnp.int32, (1, D), 1) // 64
        ct = jnp.zeros((1, D), f32)
        for h in range(HEADS):
            ct = jnp.where(head_of == h, temper[1, h] * 0.125, ct)
        scores, values = [], []
        for j in range(4):
            if j == 0:
                kv = tp[:, D:]
            else:
                kv = nt_dot(xn[2 + j], weights(1, D, 3 * D))
            k = unit(kv[:, 0:D], bd).astype(f32)
            s = head_sums_all(tq * k, bd) * ct
            if j > 0:
                s = s + jnp.where(f >= j, 0.0, BIG)
            scores.append(s)
            values.append(kv[:, D:].astype(bf16).astype(f32))
        top = jnp.maximum(
            jnp.maximum(scores[0], scores[1]), jnp.maximum(scores[2], scores[3])
        )
        es = [jnp.exp(s - top) for s in scores]
        inv = 1.0 / (es[0] + es[1] + es[2] + es[3])
        acc = jnp.zeros((ROWS, D), f32)
        for e, v in zip(es, values):
            acc = acc + (e * inv).astype(bf16).astype(f32) * v
        mix[1] = acc.astype(bf16)

    def windows():
        x0 = xn[0]
        sp = nt_dot(x0, weights(0, 0, 3 * D))
        sq = unit(sp[:, 0:D], bd)
        ones = jnp.ones((3 * ROWS, 128), bf16)

        def put(i, kv):
            kbuf[i * ROWS : (i + 1) * ROWS, :] = unit(kv[:, 0:D], bd)
            v = kv[:, D:].astype(bf16)
            for t in range(4):
                vext[i * ROWS : (i + 1) * ROWS, 256 * t : 256 * t + 128] = v[
                    :, 128 * t : 128 * t + 128
                ]

        for t in range(4):
            vext[:, 256 * t + 128 : 256 * t + 256] = ones
        put(0, sp[:, D:])

        @pl.when(plain_up)
        def _():
            copy(state, lat.at[0], LAT_DOWN, sibling).wait_recv()

        @pl.when(plain_down)
        def _():
            copy(state, lat.at[1], LAT_UP, sibling).wait_recv()

        @pl.when(cross_up)
        def _():
            copy(state.at[:, fa], lat.at[0, :, fa], LAT_DOWN, sibling).wait_recv()
            copy(state.at[:, fb], lat.at[0, :, fb], LATB, sibling).wait_recv()

        @pl.when(cross_down)
        def _():
            copy(state.at[:, fa], lat.at[1, :, fa], LAT_UP, sibling).wait_recv()
            copy(state.at[:, fb], lat.at[1, :, fb], LATB, sibling).wait_recv()

        pl.when(has_up)(lambda: normalize(1, lat.at[0]))
        pl.when(has_down)(lambda: normalize(2, lat.at[1]))
        pl.when(jnp.logical_not(has_up))(
            lambda: xn.at[1].__setitem__(Ellipsis, jnp.zeros((ROWS, D), bf16))
        )
        pl.when(jnp.logical_not(has_down))(
            lambda: xn.at[2].__setitem__(Ellipsis, jnp.zeros((ROWS, D), bf16))
        )
        for i in (1, 2):
            put(i, nt_dot(xn[i], weights(0, D, 3 * D)))

        lane = lax.broadcasted_iota(jnp.int32, (ROWS, 128), 1)
        for t in range(4):
            q = sq[:, 128 * t : 128 * t + 128]
            k = kbuf[:, 128 * t : 128 * t + 128]
            halves = []
            for e in range(2):
                qe = jnp.where((lane < 64) == (e == 0), q, jnp.zeros_like(q))
                parts = []
                for i in range(3):
                    parts.append(nt_dot(qe, k[i * ROWS : (i + 1) * ROWS]) + bias[i])
                top = jnp.maximum(
                    jnp.maximum(
                        jnp.max(parts[0], axis=1, keepdims=True),
                        jnp.max(parts[1], axis=1, keepdims=True),
                    ),
                    jnp.max(parts[2], axis=1, keepdims=True),
                )
                cs = temper[0, 2 * t + e] * 0.125
                o = jnp.zeros((ROWS, 256), f32)
                for i in range(3):
                    p = jnp.exp((parts[i] - top) * cs).astype(bf16)
                    o = o + jnp.dot(
                        p,
                        vext[i * ROWS : (i + 1) * ROWS, 256 * t : 256 * t + 256],
                        preferred_element_type=f32,
                    )
                halves.append(o[:, 0:128] / o[:, 128:256])
            mix[0, :, 128 * t : 128 * t + 128] = jnp.where(
                lane < 64, halves[0], halves[1]
            ).astype(bf16)

    def attention(i, carry):
        @pl.when(i == c)
        def _():
            for s in streams:
                s.arrive()

        pl.when(i == 1)(windows)
        pl.when(i == 0)(temporal)
        return carry

    lax.fori_loop(0, 2, attention, 0)

    fs = G[0, :, :, :, QKV:SHARD, :].reshape(D, D)
    ft = G[1, :, :, :, QKV:SHARD, :].reshape(D, D)
    update = (nt_dot(mix[0], fs) + nt_dot(mix[1], ft))[0:LON]
    lv = jnp.broadcast_to(level[...], (1, D)).astype(f32)
    step = math.log(20.0) / 16
    s0 = 0.1 * jnp.exp((lv + 1.0) * step)
    s1 = 0.1 * jnp.exp(lv * step)
    var = 1.0 + s0 * s0
    st = state[...].astype(f32)
    load_noise.wait()
    nz = noise[...].astype(f32)
    denoised = st * (1.0 / var) + (s0 * lax.rsqrt(var)) * update
    stepped = denoised + s1 * ((0.8 / s0) * (st - denoised) + 0.6 * nz)
    out[...] = jnp.where(lv == 0.0, 2.0 * nz, stepped).astype(bf16)

    for stream in streams:
        stream.finish()

    @pl.when(is_edge)
    def _():
        for cond, e in edges:
            pl.when(cond)(e.wait_send)

    pl.when(plain_down)(lat_to_down.wait_send)
    pl.when(plain_up)(lat_to_up.wait_send)

    @pl.when(cross_down)
    def _():
        hop_down.wait_send()
        a_down.wait_send()

    @pl.when(cross_up)
    def _():
        hop_up.wait_send()
        a_up.wait_send()

    pl.when(hop_in)(b_down.wait_send)
    pl.when(has_next)(time_z.wait_send)
    pl.when(c == 0)(time_sib.wait_send)

    @pl.when(has_prev)
    def _():
        copy(hist.at[1], hist.at[0], TIME_FWD, sibling).wait_send()

        @pl.when(relays)
        def _():
            copy(hist.at[1], hist.at[2], TIME_RELAY, relay_to).wait_send()


def body(
    noisy,
    perturbation,
    level,
    starts,
    tally,
    gain,
    temper,
    local_w,
    time_w,
    final_w,
):
    anyspace = pl.BlockSpec(memory_space=pl.ANY)
    smem = pl.BlockSpec(memory_space=pltpu.SMEM)
    vmem = pl.BlockSpec(memory_space=pltpu.VMEM)
    out = pl.pallas_call(
        kernel,
        out_shape=jax.ShapeDtypeStruct((LON, D), bf16),
        in_specs=[vmem] * 2 + [smem] * 2 + [anyspace] * 2 + [vmem] + [anyspace] * 3,
        out_specs=vmem,
        scratch_shapes=[
            pltpu.VMEM((2, 4, 2, 4, SHARD, D), bf16),
            pltpu.VMEM((3, LON, D), bf16),
            pltpu.VMEM((2, LON, D), bf16),
            pltpu.VMEM((6, ROWS, D), bf16),
            pltpu.VMEM((3 * ROWS, D), bf16),
            pltpu.VMEM((3 * ROWS, 2 * D), bf16),
            pltpu.VMEM((3, ROWS, ROWS), f32),
            pltpu.VMEM((LON, D // 2), bf16),
            pltpu.VMEM((2, ROWS, D), bf16),
            pltpu.VMEM((LON, D), bf16),
            pltpu.VMEM((LON, D), bf16),
            pltpu.SemaphoreType.DMA((SLOTS,)),
            pltpu.SemaphoreType.DMA((SLOTS,)),
            pltpu.SemaphoreType.DMA((4,)),
            pltpu.SemaphoreType.REGULAR((2,)),
        ],
        compiler_params=pltpu.CompilerParams(
            collective_id=0, has_side_effects=True, vmem_limit_bytes=56 * 1024 * 1024
        ),
        name="step",
    )(
        level.reshape(1, 1),
        starts.reshape(1, 1),
        tally,
        temper,
        noisy.reshape(LON, D),
        perturbation.reshape(LON, D),
        gain.reshape(1, D),
        local_w.T,
        time_w.T,
        final_w.T,
    )
    return out.reshape(noisy.shape)


def solution(mesh):
    return jax.shard_map(
        body,
        mesh=mesh,
        in_specs=(
            P("frame", "band", None, None),
            P("frame", "band", None, None),
            P("frame"),
            P("frame"),
            P(),
            P(),
            P(),
            P(None, "band"),
            P(None, "band"),
            P(None, "band"),
        ),
        out_specs=P("frame", "band", None, None),
        check_vma=False,
    )
```

```python
import math

import jax
import jax.numpy as jnp
from jax import lax
from jax.experimental import pallas as pl
from jax.experimental.pallas import tpu as pltpu
from jax.sharding import PartitionSpec as P

MESH = pl.DeviceIdType.MESH
HEADS = 8
LON = 180
WINDOW = 60
ROWS = 192
D = 512
SHARD = 64
QKV = 48
BIG = -1e30
epsilon = 1e-06
f32 = jnp.float32
bf16 = jnp.bfloat16

LAT_UP, LAT_DOWN, LATB, HOP, TIME_Z, TIME_SIB, TIME_FWD, TIME_RELAY = range(8)
EDGE = 8
NEAR = 1
MID = 1
STREAM0 = EDGE + 2 * (8 - NEAR)
PER_STREAM = 20
SLOTS = STREAM0 + 4 * PER_STREAM


def nt_dot(a, b):
    return lax.dot_general(a, b, (((1,), (1,)), ((), ())), preferred_element_type=f32)


def head_sums(x, bd):
    hi = x.astype(bf16)
    lo = (x - hi.astype(f32)).astype(bf16)
    return jnp.dot(hi, bd, preferred_element_type=f32) + jnp.dot(
        lo, bd, preferred_element_type=f32
    )


def head_sums_all(x, bd):
    return jnp.concatenate(
        [head_sums(x[:, 256 * i : 256 * i + 256], bd) for i in range(2)], axis=1
    )


def unit(u, bd):
    mean = head_sums_all(u * u, bd) * (1.0 / 64)
    return (u * lax.rsqrt(mean + epsilon)).astype(bf16)


def coords():
    f = lax.axis_index("frame")
    b = lax.axis_index("band")
    return f, b, f // 2, f % 2, b // 8, (b // 4) % 2, b % 4


def kernel(
    level,
    starts,
    tally,
    temper,
    state_in,
    noise_in,
    gain,
    local_w,
    time_w,
    final_w,
    out,
    G,
    hist,
    lat,
    xn,
    kbuf,
    vext,
    bias,
    hop,
    mix,
    state,
    noise,
    ssem,
    rsem,
    lsem,
    ready,
):
    f, b, zl, c, y, zh, x = coords()
    oc = 1 - c

    def own_copies(p, w):
        return (
            pltpu.make_async_copy(w, G.at[p, y, zh, x, pl.ds(0, QKV), :], lsem.at[0]),
            pltpu.make_async_copy(
                final_w.at[:, pl.ds(p * D, D)],
                G.at[p, y, zh, x, pl.ds(QKV, SHARD - QKV), :],
                lsem.at[1],
            ),
        )

    load_state = pltpu.make_async_copy(state_in, state, lsem.at[2])
    load_noise = pltpu.make_async_copy(noise_in, noise, lsem.at[3])
    load_state.start()
    for p, w in enumerate((local_w, time_w)):

        @pl.when(c == p)
        def _(p=p, w=w):
            for d in own_copies(p, w):
                d.start()

    def at(dx=0, dy=0, dzl=0, cc=None, zhh=None):
        yy = (y + dy + 4) % 4
        xx = (x + dx + 4) % 4
        z2 = zh if zhh is None else zhh
        c2 = c if cc is None else cc
        return {"frame": (zl + dzl) * 2 + c2, "band": (yy * 2 + z2) * 4 + xx}

    sibling = at(cc=oc)
    xr, xl, yr, yl = at(dx=1), at(dx=-1), at(dy=1), at(dy=-1)
    x2, y2 = at(dx=2), at(dy=2)

    def over_z(zz):
        return {"frame": zz * 2 + c, "band": (y * 2 + 1 - zh) * 4 + x}

    near = jnp.where(zh == 0, NEAR, 4)
    source = over_z(jnp.where(zl < near, 7, 0))
    first = jnp.where(zl == 0, jnp.where(zh == 0, 4, NEAR), 0)
    wide = jnp.where(zh == 0, 4, jnp.where(zl == 0, 8 - NEAR, NEAR))
    targets = [over_z((first + i) % 8) for i in range(8 - NEAR)]
    z_next, z_prev = at(dzl=1), at(dzl=-1)
    relay_to, relay_from = at(dzl=1, cc=0), at(dzl=-1, cc=1)
    up = {"frame": f, "band": b - 1}
    down = {"frame": f, "band": b + 1}

    has_prev, has_next = zl > 0, zl < 7
    has_up, has_down = b > 0, b < 31
    relays = (c == 1) & has_next
    relayed = (c == 0) & has_prev

    barrier = pltpu.get_barrier_semaphore()

    def greet(dev):
        pl.semaphore_signal(barrier, inc=1, device_id=dev, device_id_type=MESH)

    is_edge = (zl == 0) | (zl == 7)
    cross_up, cross_down = (x == 0) & has_up, (x == 3) & has_down
    late = zh == 1
    for dev in (sibling, xr, xl, yr, yl, x2, y2):
        greet(dev)
    count = 7
    for cond, dev in (
        (has_next, z_next),
        (has_prev, z_prev),
        (relays, relay_to),
        (relayed, relay_from),
    ):
        pl.when(cond)(lambda dev=dev: greet(dev))
        count = count + jnp.where(cond, 1, 0)
    cross = [(zh >= 0, source)]
    cross += [(is_edge & (i < wide), dev) for i, dev in enumerate(targets)]
    up2 = {"frame": f, "band": b - 2}
    down2 = {"frame": f, "band": b + 2}
    relay_up, relay_down = (x == 1) & (b > 1), (x == 2) & (b < 30)
    rows_from = [
        (cross_up, up),
        (cross_down, down),
        (cross_up, up2),
        (cross_down, down2),
    ]
    cross += rows_from + [(relay_up, up2), (relay_down, down2)]
    for cond, dev in cross:
        pl.when(cond & (zh == 0))(lambda dev=dev: greet(dev))
        count = count + jnp.where(cond & late, 1, 0)
    load_noise.start()
    load_state.wait()
    pl.semaphore_wait(barrier, count)
    for i, cond, dev in [(0, zh >= 0, source)] + [(1,) + r for r in rows_from]:

        @pl.when(cond & late)
        def _(i=i, dev=dev):
            pl.semaphore_signal(
                ready.at[i], inc=1, device_id=dev, device_id_type=MESH
            )

    for p, w in enumerate((local_w, time_w)):

        @pl.when(c == p)
        def _(p=p, w=w):
            for d in own_copies(p, w):
                d.wait()


    def copy(src, dst, slot, dev):
        return pltpu.make_async_remote_copy(
            src_ref=src,
            dst_ref=dst,
            send_sem=ssem.at[slot],
            recv_sem=rsem.at[slot],
            device_id=dev,
            device_id_type=MESH,
        )

    def gref(cc, yy, zz, xx, r0, r1):
        return G.at[cc, yy, zz, xx, pl.ds(r0, r1 - r0), :]

    lat_to_down = copy(state, lat.at[0], LAT_DOWN, down)
    lat_to_up = copy(state, lat.at[1], LAT_UP, up)
    time_z = copy(state, hist.at[1], TIME_Z, z_next)
    time_sib = copy(state, hist.at[0], TIME_SIB, sibling)

    def block(zz, i):
        return gref(c, y, zz, x, 32 * i, 32 * i + 32)

    def edge_copy(i, j):
        return pltpu.make_async_remote_copy(
            src_ref=block(zh, i),
            dst_ref=block(zh, i),
            send_sem=ssem.at[EDGE + 2 * j + i],
            recv_sem=rsem.at[EDGE + i],
            device_id=targets[j],
            device_id_type=MESH,
        )

    edges = [
        (j < wide, edge_copy(i, j)) for j in range(8 - NEAR) for i in range(2)
    ]

    def send_edges():
        for cond, e in edges:
            pl.when(cond)(e.start)

    pl.when(late & is_edge)(send_edges)

    fa, fb = pl.ds(0, D // 2), pl.ds(D // 2, D // 2)
    plain_down, plain_up = has_down & (x < 3), has_up & (x > 0)
    a_down = copy(state.at[:, fa], lat.at[0, :, fa], LAT_DOWN, down)
    a_up = copy(state.at[:, fa], lat.at[1, :, fa], LAT_UP, up)
    hop_down = copy(state.at[:, fb], hop, HOP, xl)
    hop_up = copy(state.at[:, fb], hop, HOP, xr)
    b_down = copy(hop, lat.at[0, :, fb], LATB, down2)
    b_up = copy(hop, lat.at[1, :, fb], LATB, up2)
    hop_in = relay_down | relay_up
    pl.when(cross_down)(hop_down.start)
    pl.when(cross_up)(hop_up.start)

    def start_cross():
        pl.when(cross_down)(a_down.start)
        pl.when(cross_up)(a_up.start)
        pl.when(relay_down)(b_down.start)
        pl.when(relay_up)(b_up.start)

    class Stream:
        def __init__(self, index, zz, order):
            self.s = STREAM0 + PER_STREAM * index
            self.zz, self.order = zz, order
            self.r0, self.r1 = (0, 32) if order == 0 else (32, 64)
            self.first = (xr, xl, x2) if order == 0 else (yr, yl, y2)
            self.second = (yr, yl, y2) if order == 0 else (xr, xl, x2)

        def at(self, d1, d2):
            dx, dy = (d1, d2) if self.order == 0 else (d2, d1)
            return gref(c, (y + dy + 4) % 4, self.zz, (x + dx + 4) % 4, self.r0, self.r1)

        def line(self, d2, cc):
            rows = pl.ds(self.r0, self.r1 - self.r0)
            if self.order == 0:
                return G.at[cc, (y + d2 + 4) % 4, self.zz, :, rows, :]
            return G.at[cc, :, self.zz, (x + d2 + 4) % 4, rows, :]

        def go(self, ref, slot, dev):
            copy(ref, ref, self.s + slot, dev).start()

        def got(self, ref, slot):
            copy(ref, ref, self.s + slot, sibling).wait_recv()

        def sent(self, ref, slot):
            copy(ref, ref, self.s + slot, sibling).wait_send()

        def spread(self, k, d1):
            for j in range(3):
                self.go(self.at(d1, 0), 3 + 3 * k + j, self.second[j])

        def step1(self):
            for j in range(3):
                self.go(self.at(0, 0), j, self.first[j])
            self.spread(0, 0)

        def step2(self):
            for j, d in enumerate((-1, 1, 2)):
                self.got(self.at(d, 0), j)
                self.spread(j + 1, d)
            self.go(self.line(0, c), 15, sibling)

        def step3(self):
            for j, d2 in enumerate((-1, 1, 2)):
                for k, d1 in enumerate((0, -1, 1, 2)):
                    self.got(self.at(d1, d2), 3 + 3 * k + j)
                self.go(self.line(d2, c), 16 + j, sibling)

        def arrive(self):
            for i, d in enumerate((0, -1, 1, 2)):
                self.got(self.line(d, oc), 15 + i)

        def finish(self):
            for i in range(15):
                self.sent(self.at(0, 0), i)
            for i in range(4):
                self.sent(self.line(i, c), 15 + i)

    streams = [
        Stream(0, zh, 0),
        Stream(1, zh, 1),
        Stream(2, 1 - zh, 0),
        Stream(3, 1 - zh, 1),
    ]
    mine, theirs = streams[:2], streams[2:]
    for s in mine:
        s.step1()

    def normalize(i, row_ref):
        s = row_ref[...].astype(f32)
        r = lax.rsqrt(jnp.mean(s * s, axis=-1, keepdims=True) + epsilon)
        xn[i, 0:LON, :] = (s * r * gain[...]).astype(bf16)
        xn[i, LON:ROWS, :] = jnp.zeros((ROWS - LON, D), bf16)

    normalize(0, state)

    for s in mine:
        s.step2()
    pl.when(hop_in)(hop_down.wait_recv)
    pl.when(late)(start_cross)
    pl.when(plain_down)(lat_to_down.start)
    pl.when(plain_up)(lat_to_up.start)
    pl.when(has_next)(time_z.start)
    pl.when(c == 0)(time_sib.start)

    shift = starts[...]
    qi = lax.broadcasted_iota(jnp.int32, (ROWS, ROWS), 0)
    ki = lax.broadcasted_iota(jnp.int32, (ROWS, ROWS), 1)

    def window(i):
        d = i - shift
        d = jnp.where(d < 0, d + LON, d)
        return jnp.where(d >= WINDOW, 1, 0) + jnp.where(d >= 2 * WINDOW, 1, 0)

    same = window(qi) == window(ki)
    n_above = jnp.where(has_up, tally[jnp.maximum(b - 1, 0)], 0)
    n_below = jnp.where(has_down, tally[jnp.minimum(b + 1, 31)], 0)
    n_own = tally[b]
    for i, n in enumerate((n_own, n_above, n_below)):
        seen = same & (ki < n)
        if i == 0:
            seen = seen | (qi == ki)
        bias[i] = jnp.where(seen, 0.0, BIG)

    @pl.when((zh == 0) & is_edge)
    def _():
        pl.semaphore_wait(ready.at[0], 4)
        send_edges()

    for i, s in enumerate(theirs):
        copy(block(1 - zh, i), block(1 - zh, i), EDGE + i, sibling).wait_recv()
        s.step1()

    @pl.when(has_prev)
    def _():
        copy(state, hist.at[1], TIME_Z, sibling).wait_recv()

        @pl.when(c == 1)
        def _():
            copy(hist.at[1], hist.at[0], TIME_FWD, sibling).start()

        @pl.when(c == 0)
        def _():
            copy(hist.at[1], hist.at[2], TIME_FWD, sibling).start()

        @pl.when(relays)
        def _():
            copy(hist.at[1], hist.at[2], TIME_RELAY, relay_to).start()

    @pl.when((zh == 0) & (cross_up | cross_down | hop_in))
    def _():
        pl.semaphore_wait(ready.at[1], 1)
        start_cross()

    for s in mine:
        s.step3()
    for s in theirs:
        s.step2()

    @pl.when(c == 1)
    def _():
        copy(state, hist.at[0], TIME_SIB, sibling).wait_recv()

    @pl.when(has_prev)
    def _():
        @pl.when(c == 0)
        def _():
            copy(hist.at[0], hist.at[0], TIME_FWD, sibling).wait_recv()

        @pl.when(c == 1)
        def _():
            copy(hist.at[2], hist.at[2], TIME_FWD, sibling).wait_recv()

    @pl.when((c == 0) & (zl > 1))
    def _():
        copy(hist.at[2], hist.at[2], TIME_RELAY, sibling).wait_recv()

    for j in range(3):

        @pl.when(f > j)
        def _(j=j):
            normalize(3 + j, hist.at[j])

        @pl.when(f <= j)
        def _(j=j):
            xn[3 + j] = jnp.zeros((ROWS, D), bf16)

    def own_last():
        for s in theirs:
            s.step3()

    def siblings_last():
        for s in streams:
            s.arrive()

    pl.when(c == 1)(own_last)
    pl.when(c == 0)(siblings_last)

    r_i = lax.broadcasted_iota(jnp.int32, (256, 256), 0) // 64
    c_i = lax.broadcasted_iota(jnp.int32, (256, 256), 1) // 64
    bd = jnp.where(r_i == c_i, 1.0, 0.0).astype(bf16)

    def weights(p, lo, hi):
        w = G[p, :, :, :, 0:QKV, :].reshape(32 * QKV, D)
        return w[lo:hi]

    def temporal():
        x0 = xn[0]
        tp = nt_dot(x0, weights(1, 0, 3 * D))
        tq = unit(tp[:, 0:D], bd).astype(f32)
        head_of = lax.broadcasted_iota(jnp.int32, (1, D), 1) // 64
        ct = jnp.zeros((1, D), f32)
        for h in range(HEADS):
            ct = jnp.where(head_of == h, temper[1, h] * 0.125, ct)
        scores, values = [], []
        for j in range(4):
            if j == 0:
                kv = tp[:, D:]
            else:
                kv = nt_dot(xn[2 + j], weights(1, D, 3 * D))
            k = unit(kv[:, 0:D], bd).astype(f32)
            s = head_sums_all(tq * k, bd) * ct
            if j > 0:
                s = s + jnp.where(f >= j, 0.0, BIG)
            scores.append(s)
            values.append(kv[:, D:].astype(bf16).astype(f32))
            if j == MID:
                pl.when(c == 0)(own_last)
        top = jnp.maximum(
            jnp.maximum(scores[0], scores[1]), jnp.maximum(scores[2], scores[3])
        )
        es = [jnp.exp(s - top) for s in scores]
        inv = 1.0 / (es[0] + es[1] + es[2] + es[3])
        acc = jnp.zeros((ROWS, D), f32)
        for e, v in zip(es, values):
            acc = acc + (e * inv).astype(bf16).astype(f32) * v
        mix[1] = acc.astype(bf16)

    def windows():
        x0 = xn[0]
        sp = nt_dot(x0, weights(0, 0, 3 * D))
        sq = unit(sp[:, 0:D], bd)
        ones = jnp.ones((3 * ROWS, 128), bf16)

        def put(i, kv):
            kbuf[i * ROWS : (i + 1) * ROWS, :] = unit(kv[:, 0:D], bd)
            v = kv[:, D:].astype(bf16)
            for t in range(4):
                vext[i * ROWS : (i + 1) * ROWS, 256 * t : 256 * t + 128] = v[
                    :, 128 * t : 128 * t + 128
                ]

        for t in range(4):
            vext[:, 256 * t + 128 : 256 * t + 256] = ones
        put(0, sp[:, D:])

        @pl.when(plain_up)
        def _():
            copy(state, lat.at[0], LAT_DOWN, sibling).wait_recv()

        @pl.when(plain_down)
        def _():
            copy(state, lat.at[1], LAT_UP, sibling).wait_recv()

        @pl.when(cross_up)
        def _():
            copy(state.at[:, fa], lat.at[0, :, fa], LAT_DOWN, sibling).wait_recv()
            copy(state.at[:, fb], lat.at[0, :, fb], LATB, sibling).wait_recv()

        @pl.when(cross_down)
        def _():
            copy(state.at[:, fa], lat.at[1, :, fa], LAT_UP, sibling).wait_recv()
            copy(state.at[:, fb], lat.at[1, :, fb], LATB, sibling).wait_recv()

        pl.when(has_up)(lambda: normalize(1, lat.at[0]))
        pl.when(has_down)(lambda: normalize(2, lat.at[1]))
        pl.when(jnp.logical_not(has_up))(
            lambda: xn.at[1].__setitem__(Ellipsis, jnp.zeros((ROWS, D), bf16))
        )
        pl.when(jnp.logical_not(has_down))(
            lambda: xn.at[2].__setitem__(Ellipsis, jnp.zeros((ROWS, D), bf16))
        )
        for i in (1, 2):
            put(i, nt_dot(xn[i], weights(0, D, 3 * D)))

        lane = lax.broadcasted_iota(jnp.int32, (ROWS, 128), 1)
        for t in range(4):
            q = sq[:, 128 * t : 128 * t + 128]
            k = kbuf[:, 128 * t : 128 * t + 128]
            halves = []
            for e in range(2):
                qe = jnp.where((lane < 64) == (e == 0), q, jnp.zeros_like(q))
                parts = []
                for i in range(3):
                    parts.append(nt_dot(qe, k[i * ROWS : (i + 1) * ROWS]) + bias[i])
                top = jnp.maximum(
                    jnp.maximum(
                        jnp.max(parts[0], axis=1, keepdims=True),
                        jnp.max(parts[1], axis=1, keepdims=True),
                    ),
                    jnp.max(parts[2], axis=1, keepdims=True),
                )
                cs = temper[0, 2 * t + e] * 0.125
                o = jnp.zeros((ROWS, 256), f32)
                for i in range(3):
                    p = jnp.exp((parts[i] - top) * cs).astype(bf16)
                    o = o + jnp.dot(
                        p,
                        vext[i * ROWS : (i + 1) * ROWS, 256 * t : 256 * t + 256],
                        preferred_element_type=f32,
                    )
                halves.append(o[:, 0:128] / o[:, 128:256])
            mix[0, :, 128 * t : 128 * t + 128] = jnp.where(
                lane < 64, halves[0], halves[1]
            ).astype(bf16)

    temporal()
    pl.when(c == 1)(siblings_last)
    windows()

    fs = G[0, :, :, :, QKV:SHARD, :].reshape(D, D)
    ft = G[1, :, :, :, QKV:SHARD, :].reshape(D, D)
    update = (nt_dot(mix[0], fs) + nt_dot(mix[1], ft))[0:LON]
    lv = jnp.broadcast_to(level[...], (1, D)).astype(f32)
    step = math.log(20.0) / 16
    s0 = 0.1 * jnp.exp((lv + 1.0) * step)
    s1 = 0.1 * jnp.exp(lv * step)
    var = 1.0 + s0 * s0
    st = state[...].astype(f32)
    load_noise.wait()
    nz = noise[...].astype(f32)
    denoised = st * (1.0 / var) + (s0 * lax.rsqrt(var)) * update
    stepped = denoised + s1 * ((0.8 / s0) * (st - denoised) + 0.6 * nz)
    out[...] = jnp.where(lv == 0.0, 2.0 * nz, stepped).astype(bf16)

    for stream in streams:
        stream.finish()

    @pl.when(is_edge)
    def _():
        for cond, e in edges:
            pl.when(cond)(e.wait_send)

    pl.when(plain_down)(lat_to_down.wait_send)
    pl.when(plain_up)(lat_to_up.wait_send)

    @pl.when(cross_down)
    def _():
        hop_down.wait_send()
        a_down.wait_send()

    @pl.when(cross_up)
    def _():
        hop_up.wait_send()
        a_up.wait_send()

    pl.when(hop_in)(b_down.wait_send)
    pl.when(has_next)(time_z.wait_send)
    pl.when(c == 0)(time_sib.wait_send)

    @pl.when(has_prev)
    def _():
        copy(hist.at[1], hist.at[0], TIME_FWD, sibling).wait_send()

        @pl.when(relays)
        def _():
            copy(hist.at[1], hist.at[2], TIME_RELAY, relay_to).wait_send()


def body(
    noisy,
    perturbation,
    level,
    starts,
    tally,
    gain,
    temper,
    local_w,
    time_w,
    final_w,
):
    anyspace = pl.BlockSpec(memory_space=pl.ANY)
    smem = pl.BlockSpec(memory_space=pltpu.SMEM)
    vmem = pl.BlockSpec(memory_space=pltpu.VMEM)
    out = pl.pallas_call(
        kernel,
        out_shape=jax.ShapeDtypeStruct((LON, D), bf16),
        in_specs=[vmem] * 2 + [smem] * 2 + [anyspace] * 2 + [vmem] + [anyspace] * 3,
        out_specs=vmem,
        scratch_shapes=[
            pltpu.VMEM((2, 4, 2, 4, SHARD, D), bf16),
            pltpu.VMEM((3, LON, D), bf16),
            pltpu.VMEM((2, LON, D), bf16),
            pltpu.VMEM((6, ROWS, D), bf16),
            pltpu.VMEM((3 * ROWS, D), bf16),
            pltpu.VMEM((3 * ROWS, 2 * D), bf16),
            pltpu.VMEM((3, ROWS, ROWS), f32),
            pltpu.VMEM((LON, D // 2), bf16),
            pltpu.VMEM((2, ROWS, D), bf16),
            pltpu.VMEM((LON, D), bf16),
            pltpu.VMEM((LON, D), bf16),
            pltpu.SemaphoreType.DMA((SLOTS,)),
            pltpu.SemaphoreType.DMA((SLOTS,)),
            pltpu.SemaphoreType.DMA((4,)),
            pltpu.SemaphoreType.REGULAR((2,)),
        ],
        compiler_params=pltpu.CompilerParams(
            collective_id=0, has_side_effects=True, vmem_limit_bytes=56 * 1024 * 1024
        ),
        name="step",
    )(
        level.reshape(1, 1),
        starts.reshape(1, 1),
        tally,
        temper,
        noisy.reshape(LON, D),
        perturbation.reshape(LON, D),
        gain.reshape(1, D),
        local_w.T,
        time_w.T,
        final_w.T,
    )
    return out.reshape(noisy.shape)


def solution(mesh):
    return jax.shard_map(
        body,
        mesh=mesh,
        in_specs=(
            P("frame", "band", None, None),
            P("frame", "band", None, None),
            P("frame"),
            P("frame"),
            P(),
            P(),
            P(),
            P(None, "band"),
            P(None, "band"),
            P(None, "band"),
        ),
        out_specs=P("frame", "band", None, None),
        check_vma=False,
    )
```

```python
import math

import jax
import jax.numpy as jnp
from jax import lax
from jax.experimental import pallas as pl
from jax.experimental.pallas import tpu as pltpu
from jax.sharding import PartitionSpec as P

MESH = pl.DeviceIdType.MESH
HEADS = 8
LON = 180
WINDOW = 60
ROWS = 192
D = 512
SHARD = 64
QKV = 48
BIG = -1e30
epsilon = 1e-06
f32 = jnp.float32
bf16 = jnp.bfloat16

LAT_UP, LAT_DOWN, LATB, HOP, TIME_Z, TIME_SIB, TIME_FWD, TIME_RELAY = range(8)
EDGE = 8
NEAR = 1
MID = 1
STREAM0 = EDGE + 2 * (8 - NEAR)
PER_STREAM = 20
SLOTS = STREAM0 + 4 * PER_STREAM


def nt_dot(a, b):
    return lax.dot_general(a, b, (((1,), (1,)), ((), ())), preferred_element_type=f32)


def head_sums(x, bd):
    hi = x.astype(bf16)
    lo = (x - hi.astype(f32)).astype(bf16)
    return jnp.dot(hi, bd, preferred_element_type=f32) + jnp.dot(
        lo, bd, preferred_element_type=f32
    )


def head_sums_all(x, bd):
    return jnp.concatenate(
        [head_sums(x[:, 256 * i : 256 * i + 256], bd) for i in range(2)], axis=1
    )


def unit(u, bd):
    mean = head_sums_all(u * u, bd) * (1.0 / 64)
    return (u * lax.rsqrt(mean + epsilon)).astype(bf16)


def coords():
    f = lax.axis_index("frame")
    b = lax.axis_index("band")
    return f, b, f // 2, f % 2, b // 8, (b // 4) % 2, b % 4


def kernel(
    level,
    starts,
    tally,
    temper,
    state_in,
    noise_in,
    gain,
    local_w,
    time_w,
    final_w,
    out,
    G,
    hist,
    lat,
    xn,
    kbuf,
    vext,
    bias,
    hop,
    mix,
    state,
    noise,
    ssem,
    rsem,
    lsem,
    ready,
):
    f, b, zl, c, y, zh, x = coords()
    oc = 1 - c

    def own_copies(p, w):
        return (
            pltpu.make_async_copy(w, G.at[p, y, zh, x, pl.ds(0, QKV), :], lsem.at[0]),
            pltpu.make_async_copy(
                final_w.at[:, pl.ds(p * D, D)],
                G.at[p, y, zh, x, pl.ds(QKV, SHARD - QKV), :],
                lsem.at[1],
            ),
        )

    load_state = pltpu.make_async_copy(state_in, state, lsem.at[2])
    load_noise = pltpu.make_async_copy(noise_in, noise, lsem.at[3])
    load_state.start()
    for p, w in enumerate((local_w, time_w)):

        @pl.when(c == p)
        def _(p=p, w=w):
            for d in own_copies(p, w):
                d.start()

    def at(dx=0, dy=0, dzl=0, cc=None, zhh=None):
        yy = (y + dy + 4) % 4
        xx = (x + dx + 4) % 4
        z2 = zh if zhh is None else zhh
        c2 = c if cc is None else cc
        return {"frame": (zl + dzl) * 2 + c2, "band": (yy * 2 + z2) * 4 + xx}

    sibling = at(cc=oc)
    xr, xl, yr, yl = at(dx=1), at(dx=-1), at(dy=1), at(dy=-1)
    x2, y2 = at(dx=2), at(dy=2)

    def over_z(zz):
        return {"frame": zz * 2 + c, "band": (y * 2 + 1 - zh) * 4 + x}

    near = jnp.where(zh == 0, NEAR, 4)
    source = over_z(jnp.where(zl < near, 7, 0))
    first = jnp.where(zl == 0, jnp.where(zh == 0, 4, NEAR), 0)
    wide = jnp.where(zh == 0, 4, jnp.where(zl == 0, 8 - NEAR, NEAR))
    targets = [over_z((first + i) % 8) for i in range(8 - NEAR)]
    z_next, z_prev = at(dzl=1), at(dzl=-1)
    relay_to, relay_from = at(dzl=1, cc=0), at(dzl=-1, cc=1)
    up = {"frame": f, "band": b - 1}
    down = {"frame": f, "band": b + 1}

    has_prev, has_next = zl > 0, zl < 7
    has_up, has_down = b > 0, b < 31
    relays = (c == 1) & has_next
    relayed = (c == 0) & has_prev

    barrier = pltpu.get_barrier_semaphore()

    def greet(dev):
        pl.semaphore_signal(barrier, inc=1, device_id=dev, device_id_type=MESH)

    is_edge = (zl == 0) | (zl == 7)
    cross_up, cross_down = (x == 0) & has_up, (x == 3) & has_down
    late = zh == 1
    for dev in (sibling, xr, xl, yr, yl, x2, y2):
        greet(dev)
    count = 7
    for cond, dev in (
        (has_next, z_next),
        (has_prev, z_prev),
        (relays, relay_to),
        (relayed, relay_from),
    ):
        pl.when(cond)(lambda dev=dev: greet(dev))
        count = count + jnp.where(cond, 1, 0)
    cross = [(zh >= 0, source)]
    cross += [(is_edge & (i < wide), dev) for i, dev in enumerate(targets)]
    up2 = {"frame": f, "band": b - 2}
    down2 = {"frame": f, "band": b + 2}
    relay_up, relay_down = (x == 1) & (b > 1), (x == 2) & (b < 30)
    rows_from = [
        (cross_up, up),
        (cross_down, down),
        (cross_up, up2),
        (cross_down, down2),
    ]
    cross += rows_from + [(relay_up, up2), (relay_down, down2)]
    for cond, dev in cross:
        pl.when(cond & (zh == 0))(lambda dev=dev: greet(dev))
        count = count + jnp.where(cond & late, 1, 0)
    load_noise.start()
    load_state.wait()
    pl.semaphore_wait(barrier, count)
    for i, cond, dev in [(0, zh >= 0, source)] + [(1,) + r for r in rows_from]:

        @pl.when(cond & late)
        def _(i=i, dev=dev):
            pl.semaphore_signal(
                ready.at[i], inc=1, device_id=dev, device_id_type=MESH
            )

    for p, w in enumerate((local_w, time_w)):

        @pl.when(c == p)
        def _(p=p, w=w):
            for d in own_copies(p, w):
                d.wait()


    def copy(src, dst, slot, dev):
        return pltpu.make_async_remote_copy(
            src_ref=src,
            dst_ref=dst,
            send_sem=ssem.at[slot],
            recv_sem=rsem.at[slot],
            device_id=dev,
            device_id_type=MESH,
        )

    def gref(cc, yy, zz, xx, r0, r1):
        return G.at[cc, yy, zz, xx, pl.ds(r0, r1 - r0), :]

    lat_to_down = copy(state, lat.at[0], LAT_DOWN, down)
    lat_to_up = copy(state, lat.at[1], LAT_UP, up)
    time_z = copy(state, hist.at[1], TIME_Z, z_next)
    time_sib = copy(state, hist.at[0], TIME_SIB, sibling)

    def block(zz, i):
        return gref(c, y, zz, x, 32 * i, 32 * i + 32)

    def edge_copy(i, j):
        return pltpu.make_async_remote_copy(
            src_ref=block(zh, i),
            dst_ref=block(zh, i),
            send_sem=ssem.at[EDGE + 2 * j + i],
            recv_sem=rsem.at[EDGE + i],
            device_id=targets[j],
            device_id_type=MESH,
        )

    edges = [
        (j < wide, edge_copy(i, j)) for j in range(8 - NEAR) for i in range(2)
    ]

    def send_edges():
        for cond, e in edges:
            pl.when(cond)(e.start)

    pl.when(late & is_edge)(send_edges)

    fa, fb = pl.ds(0, D // 2), pl.ds(D // 2, D // 2)
    plain_down, plain_up = has_down & (x < 3), has_up & (x > 0)
    a_down = copy(state.at[:, fa], lat.at[0, :, fa], LAT_DOWN, down)
    a_up = copy(state.at[:, fa], lat.at[1, :, fa], LAT_UP, up)
    hop_down = copy(state.at[:, fb], hop, HOP, xl)
    hop_up = copy(state.at[:, fb], hop, HOP, xr)
    b_down = copy(hop, lat.at[0, :, fb], LATB, down2)
    b_up = copy(hop, lat.at[1, :, fb], LATB, up2)
    hop_in = relay_down | relay_up
    pl.when(cross_down)(hop_down.start)
    pl.when(cross_up)(hop_up.start)

    def start_cross():
        pl.when(cross_down)(a_down.start)
        pl.when(cross_up)(a_up.start)
        pl.when(relay_down)(b_down.start)
        pl.when(relay_up)(b_up.start)

    class Stream:
        def __init__(self, index, zz, order):
            self.s = STREAM0 + PER_STREAM * index
            self.zz, self.order = zz, order
            self.r0, self.r1 = (0, 32) if order == 0 else (32, 64)
            self.first = (xr, xl, x2) if order == 0 else (yr, yl, y2)
            self.second = (yr, yl, y2) if order == 0 else (xr, xl, x2)

        def at(self, d1, d2):
            dx, dy = (d1, d2) if self.order == 0 else (d2, d1)
            return gref(c, (y + dy + 4) % 4, self.zz, (x + dx + 4) % 4, self.r0, self.r1)

        def line(self, d2, cc):
            rows = pl.ds(self.r0, self.r1 - self.r0)
            if self.order == 0:
                return G.at[cc, (y + d2 + 4) % 4, self.zz, :, rows, :]
            return G.at[cc, :, self.zz, (x + d2 + 4) % 4, rows, :]

        def go(self, ref, slot, dev):
            copy(ref, ref, self.s + slot, dev).start()

        def got(self, ref, slot):
            copy(ref, ref, self.s + slot, sibling).wait_recv()

        def sent(self, ref, slot):
            copy(ref, ref, self.s + slot, sibling).wait_send()

        def spread(self, k, d1):
            for j in range(3):
                self.go(self.at(d1, 0), 3 + 3 * k + j, self.second[j])

        def step1(self):
            for j in range(3):
                self.go(self.at(0, 0), j, self.first[j])
            self.spread(0, 0)

        def step2(self):
            for j, d in enumerate((-1, 1, 2)):
                self.got(self.at(d, 0), j)
                self.spread(j + 1, d)
            self.go(self.line(0, c), 15, sibling)

        def step3(self):
            for j, d2 in enumerate((-1, 1, 2)):
                for k, d1 in enumerate((0, -1, 1, 2)):
                    self.got(self.at(d1, d2), 3 + 3 * k + j)
                self.go(self.line(d2, c), 16 + j, sibling)

        def arrive(self):
            for i, d in enumerate((0, -1, 1, 2)):
                self.got(self.line(d, oc), 15 + i)

        def finish(self):
            for i in range(15):
                self.sent(self.at(0, 0), i)
            for i in range(4):
                self.sent(self.line(i, c), 15 + i)

    streams = [
        Stream(0, zh, 0),
        Stream(1, zh, 1),
        Stream(2, 1 - zh, 0),
        Stream(3, 1 - zh, 1),
    ]
    mine, theirs = streams[:2], streams[2:]
    for s in mine:
        s.step1()

    def normalize(i, row_ref):
        s = row_ref[...].astype(f32)
        r = lax.rsqrt(jnp.mean(s * s, axis=-1, keepdims=True) + epsilon)
        xn[i, 0:LON, :] = (s * r * gain[...]).astype(bf16)
        xn[i, LON:ROWS, :] = jnp.zeros((ROWS - LON, D), bf16)

    normalize(0, state)

    for s in mine:
        s.step2()
    pl.when(hop_in)(hop_down.wait_recv)
    pl.when(late)(start_cross)
    pl.when(plain_down)(lat_to_down.start)
    pl.when(plain_up)(lat_to_up.start)
    pl.when(has_next)(time_z.start)
    pl.when(c == 0)(time_sib.start)

    shift = starts[...]
    qi = lax.broadcasted_iota(jnp.int32, (ROWS, ROWS), 0)
    ki = lax.broadcasted_iota(jnp.int32, (ROWS, ROWS), 1)

    def window(i):
        d = i - shift
        d = jnp.where(d < 0, d + LON, d)
        return jnp.where(d >= WINDOW, 1, 0) + jnp.where(d >= 2 * WINDOW, 1, 0)

    same = window(qi) == window(ki)
    n_above = jnp.where(has_up, tally[jnp.maximum(b - 1, 0)], 0)
    n_below = jnp.where(has_down, tally[jnp.minimum(b + 1, 31)], 0)
    n_own = tally[b]
    for i, n in enumerate((n_own, n_above, n_below)):
        seen = same & (ki < n)
        if i == 0:
            seen = seen | (qi == ki)
        bias[i] = jnp.where(seen, 0.0, BIG)

    @pl.when((zh == 0) & is_edge)
    def _():
        pl.semaphore_wait(ready.at[0], 4)
        send_edges()

    for i, s in enumerate(theirs):
        copy(block(1 - zh, i), block(1 - zh, i), EDGE + i, sibling).wait_recv()
        s.step1()

    @pl.when(has_prev)
    def _():
        copy(state, hist.at[1], TIME_Z, sibling).wait_recv()

        @pl.when(c == 1)
        def _():
            copy(hist.at[1], hist.at[0], TIME_FWD, sibling).start()

        @pl.when(c == 0)
        def _():
            copy(hist.at[1], hist.at[2], TIME_FWD, sibling).start()

        @pl.when(relays)
        def _():
            copy(hist.at[1], hist.at[2], TIME_RELAY, relay_to).start()

    @pl.when((zh == 0) & (cross_up | cross_down | hop_in))
    def _():
        pl.semaphore_wait(ready.at[1], 1)
        start_cross()

    for s in mine:
        s.step3()
    for s in theirs:
        s.step2()

    @pl.when(c == 1)
    def _():
        copy(state, hist.at[0], TIME_SIB, sibling).wait_recv()

    @pl.when(has_prev)
    def _():
        @pl.when(c == 0)
        def _():
            copy(hist.at[0], hist.at[0], TIME_FWD, sibling).wait_recv()

        @pl.when(c == 1)
        def _():
            copy(hist.at[2], hist.at[2], TIME_FWD, sibling).wait_recv()

    @pl.when((c == 0) & (zl > 1))
    def _():
        copy(hist.at[2], hist.at[2], TIME_RELAY, sibling).wait_recv()

    for j in range(3):

        @pl.when(f > j)
        def _(j=j):
            normalize(3 + j, hist.at[j])

        @pl.when(f <= j)
        def _(j=j):
            xn[3 + j] = jnp.zeros((ROWS, D), bf16)

    def own_last():
        for s in theirs:
            s.step3()

    def siblings_last():
        for s in streams:
            s.arrive()

    @pl.when(plain_up)
    def _():
        copy(state, lat.at[0], LAT_DOWN, sibling).wait_recv()
        normalize(1, lat.at[0])

    @pl.when(plain_down)
    def _():
        copy(state, lat.at[1], LAT_UP, sibling).wait_recv()
        normalize(2, lat.at[1])

    @pl.when(jnp.logical_not(has_up))
    def _():
        xn[1] = jnp.zeros((ROWS, D), bf16)

    @pl.when(jnp.logical_not(has_down))
    def _():
        xn[2] = jnp.zeros((ROWS, D), bf16)

    pl.when(c == 1)(own_last)
    pl.when(c == 0)(siblings_last)

    r_i = lax.broadcasted_iota(jnp.int32, (256, 256), 0) // 64
    c_i = lax.broadcasted_iota(jnp.int32, (256, 256), 1) // 64
    bd = jnp.where(r_i == c_i, 1.0, 0.0).astype(bf16)

    def weights(p, lo, hi):
        w = G[p, :, :, :, 0:QKV, :].reshape(32 * QKV, D)
        return w[lo:hi]

    def temporal():
        x0 = xn[0]
        tp = nt_dot(x0, weights(1, 0, 3 * D))
        tq = unit(tp[:, 0:D], bd).astype(f32)
        head_of = lax.broadcasted_iota(jnp.int32, (1, D), 1) // 64
        ct = jnp.zeros((1, D), f32)
        for h in range(HEADS):
            ct = jnp.where(head_of == h, temper[1, h] * 0.125, ct)
        scores, values = [], []
        for j in range(4):
            if j == 0:
                kv = tp[:, D:]
            else:
                kv = nt_dot(xn[2 + j], weights(1, D, 3 * D))
            k = unit(kv[:, 0:D], bd).astype(f32)
            s = head_sums_all(tq * k, bd) * ct
            if j > 0:
                s = s + jnp.where(f >= j, 0.0, BIG)
            scores.append(s)
            values.append(kv[:, D:].astype(bf16).astype(f32))
            if j == MID:
                pl.when(c == 0)(own_last)
        top = jnp.maximum(
            jnp.maximum(scores[0], scores[1]), jnp.maximum(scores[2], scores[3])
        )
        es = [jnp.exp(s - top) for s in scores]
        inv = 1.0 / (es[0] + es[1] + es[2] + es[3])
        acc = jnp.zeros((ROWS, D), f32)
        for e, v in zip(es, values):
            acc = acc + (e * inv).astype(bf16).astype(f32) * v
        mix[1] = acc.astype(bf16)

    def windows():
        x0 = xn[0]
        sp = nt_dot(x0, weights(0, 0, 3 * D))
        sq = unit(sp[:, 0:D], bd)
        ones = jnp.ones((3 * ROWS, 128), bf16)

        def put(i, kv):
            kbuf[i * ROWS : (i + 1) * ROWS, :] = unit(kv[:, 0:D], bd)
            v = kv[:, D:].astype(bf16)
            for t in range(4):
                vext[i * ROWS : (i + 1) * ROWS, 256 * t : 256 * t + 128] = v[
                    :, 128 * t : 128 * t + 128
                ]

        for t in range(4):
            vext[:, 256 * t + 128 : 256 * t + 256] = ones
        put(0, sp[:, D:])

        @pl.when(cross_up)
        def _():
            copy(state.at[:, fa], lat.at[0, :, fa], LAT_DOWN, sibling).wait_recv()
            copy(state.at[:, fb], lat.at[0, :, fb], LATB, sibling).wait_recv()

        @pl.when(cross_down)
        def _():
            copy(state.at[:, fa], lat.at[1, :, fa], LAT_UP, sibling).wait_recv()
            copy(state.at[:, fb], lat.at[1, :, fb], LATB, sibling).wait_recv()

        pl.when(cross_up)(lambda: normalize(1, lat.at[0]))
        pl.when(cross_down)(lambda: normalize(2, lat.at[1]))
        for i in (1, 2):
            put(i, nt_dot(xn[i], weights(0, D, 3 * D)))

        lane = lax.broadcasted_iota(jnp.int32, (ROWS, 128), 1)
        for t in range(4):
            q = sq[:, 128 * t : 128 * t + 128]
            k = kbuf[:, 128 * t : 128 * t + 128]
            halves = []
            for e in range(2):
                qe = jnp.where((lane < 64) == (e == 0), q, jnp.zeros_like(q))
                parts = []
                for i in range(3):
                    parts.append(nt_dot(qe, k[i * ROWS : (i + 1) * ROWS]) + bias[i])
                top = jnp.maximum(
                    jnp.maximum(
                        jnp.max(parts[0], axis=1, keepdims=True),
                        jnp.max(parts[1], axis=1, keepdims=True),
                    ),
                    jnp.max(parts[2], axis=1, keepdims=True),
                )
                cs = temper[0, 2 * t + e] * 0.125
                o = jnp.zeros((ROWS, 256), f32)
                for i in range(3):
                    p = jnp.exp((parts[i] - top) * cs).astype(bf16)
                    o = o + jnp.dot(
                        p,
                        vext[i * ROWS : (i + 1) * ROWS, 256 * t : 256 * t + 256],
                        preferred_element_type=f32,
                    )
                halves.append(o[:, 0:128] / o[:, 128:256])
            mix[0, :, 128 * t : 128 * t + 128] = jnp.where(
                lane < 64, halves[0], halves[1]
            ).astype(bf16)

    temporal()
    pl.when(c == 1)(siblings_last)
    windows()

    fs = G[0, :, :, :, QKV:SHARD, :].reshape(D, D)
    ft = G[1, :, :, :, QKV:SHARD, :].reshape(D, D)
    update = (nt_dot(mix[0], fs) + nt_dot(mix[1], ft))[0:LON]
    lv = jnp.broadcast_to(level[...], (1, D)).astype(f32)
    step = math.log(20.0) / 16
    s0 = 0.1 * jnp.exp((lv + 1.0) * step)
    s1 = 0.1 * jnp.exp(lv * step)
    var = 1.0 + s0 * s0
    st = state[...].astype(f32)
    load_noise.wait()
    nz = noise[...].astype(f32)
    denoised = st * (1.0 / var) + (s0 * lax.rsqrt(var)) * update
    stepped = denoised + s1 * ((0.8 / s0) * (st - denoised) + 0.6 * nz)
    out[...] = jnp.where(lv == 0.0, 2.0 * nz, stepped).astype(bf16)

    for stream in streams:
        stream.finish()

    @pl.when(is_edge)
    def _():
        for cond, e in edges:
            pl.when(cond)(e.wait_send)

    pl.when(plain_down)(lat_to_down.wait_send)
    pl.when(plain_up)(lat_to_up.wait_send)

    @pl.when(cross_down)
    def _():
        hop_down.wait_send()
        a_down.wait_send()

    @pl.when(cross_up)
    def _():
        hop_up.wait_send()
        a_up.wait_send()

    pl.when(hop_in)(b_down.wait_send)
    pl.when(has_next)(time_z.wait_send)
    pl.when(c == 0)(time_sib.wait_send)

    @pl.when(has_prev)
    def _():
        copy(hist.at[1], hist.at[0], TIME_FWD, sibling).wait_send()

        @pl.when(relays)
        def _():
            copy(hist.at[1], hist.at[2], TIME_RELAY, relay_to).wait_send()


def body(
    noisy,
    perturbation,
    level,
    starts,
    tally,
    gain,
    temper,
    local_w,
    time_w,
    final_w,
):
    anyspace = pl.BlockSpec(memory_space=pl.ANY)
    smem = pl.BlockSpec(memory_space=pltpu.SMEM)
    vmem = pl.BlockSpec(memory_space=pltpu.VMEM)
    out = pl.pallas_call(
        kernel,
        out_shape=jax.ShapeDtypeStruct((LON, D), bf16),
        in_specs=[vmem] * 2 + [smem] * 2 + [anyspace] * 2 + [vmem] + [anyspace] * 3,
        out_specs=vmem,
        scratch_shapes=[
            pltpu.VMEM((2, 4, 2, 4, SHARD, D), bf16),
            pltpu.VMEM((3, LON, D), bf16),
            pltpu.VMEM((2, LON, D), bf16),
            pltpu.VMEM((6, ROWS, D), bf16),
            pltpu.VMEM((3 * ROWS, D), bf16),
            pltpu.VMEM((3 * ROWS, 2 * D), bf16),
            pltpu.VMEM((3, ROWS, ROWS), f32),
            pltpu.VMEM((LON, D // 2), bf16),
            pltpu.VMEM((2, ROWS, D), bf16),
            pltpu.VMEM((LON, D), bf16),
            pltpu.VMEM((LON, D), bf16),
            pltpu.SemaphoreType.DMA((SLOTS,)),
            pltpu.SemaphoreType.DMA((SLOTS,)),
            pltpu.SemaphoreType.DMA((4,)),
            pltpu.SemaphoreType.REGULAR((2,)),
        ],
        compiler_params=pltpu.CompilerParams(
            collective_id=0, has_side_effects=True, vmem_limit_bytes=56 * 1024 * 1024
        ),
        name="step",
    )(
        level.reshape(1, 1),
        starts.reshape(1, 1),
        tally,
        temper,
        noisy.reshape(LON, D),
        perturbation.reshape(LON, D),
        gain.reshape(1, D),
        local_w.T,
        time_w.T,
        final_w.T,
    )
    return out.reshape(noisy.shape)


def solution(mesh):
    return jax.shard_map(
        body,
        mesh=mesh,
        in_specs=(
            P("frame", "band", None, None),
            P("frame", "band", None, None),
            P("frame"),
            P("frame"),
            P(),
            P(),
            P(),
            P(None, "band"),
            P(None, "band"),
            P(None, "band"),
        ),
        out_specs=P("frame", "band", None, None),
        check_vma=False,
    )
```
